128 devices in a mesh: wall: 32 (over y, x, core), surf: 4 (over z).
Axes of the slice: x: 4, y: 4, z: 4, core: 2. Of those that a mesh axis runs over, the one named last changes fastest.
Arguments:
- state: bfloat16 [8192, 162], P(('wall', 'surf')), may hold values from -6 to 6
- source: bfloat16 [8192, 162], P(('wall', 'surf')), may hold values from -6 to 6
- face_coef: float32 [8192, 4], P(('wall', 'surf')), may hold values from 0.1 to 0.5
- neighbour: int32 [8192, 4], P(('wall', 'surf')), may hold values from 0 to 191
- lift: bfloat16 [162, 162], replicated, may hold values from -0.5 to 0.5
- elem_slot: int32 [64, 128], P('wall', 'surf'), may hold values from 0 to 63, as said below
- line_len: int32 [128], P('surf'), may hold values from 32 to 64
- dinv: bfloat16 [64, 128, 162, 162], P('wall', 'surf'), may hold values from -0.3 to 1.2
- lower: bfloat16 [64, 128, 162, 162], P('wall', 'surf'), may hold values from -1.4 to 0.4
- upper: bfloat16 [64, 128, 162, 162], P('wall', 'surf'), may hold values from -0.4 to 1.4
Outputs:
- solution: float32 [64, 128, 162], P('wall', 'surf')
The draws below stay inside these ranges and needn't reach their ends.
Inputs may be any that keep to these rules, and one draw needn't show every extreme that they name: `elem_slot`: on each device the entries form a permutation of its 64 slots.
All inputs are finite; a program needn't handle non-finite values.
Results may differ from the reference program's by a relative error of at most 0.0023.
Values may be sent and summed in bfloat16 or wider, within the bound.
A program may use at most 128 MiB of HBM per device.

```python
import math
import jax
import jax.numpy as jnp
from jax import lax

B = 162
F = 4
E_DEV = 2
LINES = 32
SLOTS = 64
CELLS_PER_STRAND = 64
STRAND_COUNT = 128
ROWS = 8192
N_SURF = 4


def draw_neighbour(key, part):
    key_a = jax.random.fold_in(key, 11)
    key_b = jax.random.fold_in(key, 12)
    pick = jax.random.randint(key_a, (ROWS, F), 0, 4)
    side = pick - (pick >= 2).astype(jnp.int32)
    slot_there = jax.random.randint(key_b, (ROWS, F), 0, SLOTS)
    values = (side * SLOTS + slot_there).astype(jnp.int32)
    values = values.at[0, 0].set(3 * SLOTS - 1)
    values = values.at[1, 0].set(0)
    return values


def draw_elem_slot(key, part):
    count = CELLS_PER_STRAND // E_DEV * (STRAND_COUNT // LINES)
    keys = jax.random.split(jax.random.fold_in(key, 21), count)
    perms = jax.vmap(lambda single: jax.random.permutation(single, SLOTS))(keys)
    perms = perms.reshape(CELLS_PER_STRAND // E_DEV, STRAND_COUNT // LINES, E_DEV, LINES)
    perms = jnp.transpose(perms, (0, 2, 1, 3)).reshape(CELLS_PER_STRAND, STRAND_COUNT)
    return perms.astype(jnp.int32)


def draw_line_len(key, part):
    values = jax.random.randint(jax.random.fold_in(key, 31), (STRAND_COUNT,), CELLS_PER_STRAND // 2, CELLS_PER_STRAND + 1)
    return values.at[0].set(CELLS_PER_STRAND).astype(jnp.int32)


def draw_dinv(key, part):
    key_d = jax.random.fold_in(key, 41)
    key_n = jax.random.fold_in(key, 42)
    shape = (CELLS_PER_STRAND, STRAND_COUNT, B, B)
    central_submatrix = jax.random.uniform(key_d, (CELLS_PER_STRAND, STRAND_COUNT, B), jnp.float32, 0.88, 0.92)
    noise = jnp.clip(jax.random.normal(key_n, shape, jnp.float32), -4.0, 4.0)
    values = central_submatrix[..., None] * jnp.eye(B, dtype=jnp.float32) + noise * (0.2 / B ** 0.5)
    return values.astype(jnp.bfloat16)


def coupling(base, noise, slow_share, sign):
    key_s = jax.random.fold_in(base, 1)
    key_f = jax.random.fold_in(base, 2)
    key_p = jax.random.fold_in(base, 3)
    key_c = jax.random.fold_in(base, 4)
    slow = jax.random.uniform(key_s, (STRAND_COUNT, B), jnp.float32) < slow_share
    fast = jax.random.uniform(key_f, (CELLS_PER_STRAND, STRAND_COUNT, B), jnp.float32, 0.3, 0.75)
    relaxation_factor = jnp.where(slow[None, :, :], 0.97, fast)
    cell_locations = jax.random.randint(key_p, (3, STRAND_COUNT), 0, CELLS_PER_STRAND)
    split_positions = jax.random.uniform(key_c, (3, STRAND_COUNT), jnp.float32, 0.5, 0.8)
    location_array = jnp.arange(CELLS_PER_STRAND, dtype=jnp.int32)[:, None]
    segment_span = jnp.ones((CELLS_PER_STRAND, STRAND_COUNT), jnp.float32)
    for chosen_entry in range(3):
        segment_span = segment_span * jnp.where(location_array == cell_locations[chosen_entry][None, :], split_positions[chosen_entry][None, :], 1.0)
    central_submatrix = relaxation_factor * segment_span[:, :, None] / 0.9
    values = central_submatrix[..., None] * jnp.eye(B, dtype=jnp.float32) + noise * (0.25 / B ** 0.5)
    return (sign * values).astype(jnp.bfloat16)


def draw_lower(key, part):
    base = jax.random.fold_in(key, 51)
    key_n = jax.random.fold_in(base, 9)
    shape = (CELLS_PER_STRAND, STRAND_COUNT, B, B)
    noise = jnp.clip(jax.random.normal(key_n, shape, jnp.float32), -4.0, 4.0)
    share = 0.5
    return coupling(base, noise, share, -1.0)


def draw_upper(key, part):
    base = jax.random.fold_in(key, 61)
    key_n = jax.random.fold_in(base, 9)
    shape = (CELLS_PER_STRAND, STRAND_COUNT, B, B)
    noise = jnp.clip(jax.random.normal(key_n, shape, jnp.float32), -4.0, 4.0)
    share = 0.5
    return coupling(base, noise, share, 1.0)


def steps_of(rng, extent, cuts, low, largest):
    factor_of, own = 1.0, jax.random.fold_in(rng, 6)
    for dim, shards_of in cuts:
        heights = jnp.exp(jax.random.uniform(jax.random.fold_in(own, dim), (shards_of,), jnp.float32, low / len(cuts), largest / len(cuts)))
        factor_of = factor_of * jnp.repeat(heights, extent[dim] // shards_of).reshape([-1 if axis == dim else 1 for axis in range(len(extent))])
    return factor_of


def normal_values(key, dims, spread, most, pieces=(), kind=jnp.bfloat16):
    values = spread * jax.random.normal(key, dims, jnp.float32)
    if pieces:
        values = values * steps_of(key, dims, pieces, -0.22, 0.18)
    return jnp.clip(values, -most, most).astype(kind)


def setup_inputs(seed: int = 0) -> dict:
    streams_of = jax.random.split(jax.random.key(seed), 11)
    return {
        "state": normal_values(streams_of[0], (ROWS, B), 1.0, 6.0, ((0, 128),)),
        "source": normal_values(streams_of[1], (ROWS, B), 1.0, 6.0, ((0, 128),)),
        "face_coef": jnp.clip(jnp.exp(math.log(0.5) - 1.609438 * jax.random.uniform(streams_of[2], (ROWS, F), jnp.float32) ** steps_of(streams_of[2], (ROWS, F), ((0, 128),), -0.2, 0.2)), 0.1, 0.5),
        "neighbour": draw_neighbour(jax.random.fold_in(streams_of[10], 71), 0),
        "lift": normal_values(streams_of[4], (B, B), B ** -0.5, 0.5),
        "elem_slot": draw_elem_slot(jax.random.fold_in(streams_of[10], 71), 0),
        "line_len": draw_line_len(jax.random.fold_in(streams_of[10], 71), 0),
        "dinv": draw_dinv(jax.random.fold_in(streams_of[10], 71), 0),
        "lower": draw_lower(jax.random.fold_in(streams_of[10], 71), 0),
        "upper": draw_upper(jax.random.fold_in(streams_of[10], 71), 0),
    }


def apply_block(matrix, vector):
    return jnp.einsum("lij,lj->li", matrix.astype(jnp.float32), vector, precision=lax.Precision.HIGHEST)


def reference(state, source, face_coef, neighbour, lift, elem_slot, line_len, dinv, lower, upper):
    rows = jnp.arange(ROWS, dtype=jnp.int32)
    device = rows // SLOTS
    wall_pos = device // N_SURF
    surf_pos = device % N_SURF
    offset = neighbour // SLOTS - 1
    slot_there = neighbour % SLOTS
    nbrow = ((wall_pos[:, None] * N_SURF + (surf_pos[:, None] + offset) % N_SURF) * SLOTS + slot_there).astype(jnp.int32)
    nb_vals = state[nbrow].astype(jnp.float32)
    face_sum = jnp.sum(face_coef[:, :, None] * (state.astype(jnp.float32)[:, None, :] - nb_vals), axis=1).astype(jnp.bfloat16)
    residual = source.astype(jnp.float32) - jnp.dot(face_sum, lift, preferred_element_type=jnp.float32)
    gpos = jnp.arange(CELLS_PER_STRAND, dtype=jnp.int32)[:, None]
    lpos = jnp.arange(STRAND_COUNT, dtype=jnp.int32)[None, :]
    row_of = (((gpos // E_DEV) * N_SURF + lpos // LINES) * SLOTS + elem_slot).astype(jnp.int32)
    line_rhs = residual[row_of]
    active = (gpos < line_len[None, :]).astype(jnp.float32)

    def forward(carried, items):
        dblock, lblock, rhs_now, act_now = items
        value = act_now[:, None] * apply_block(dblock, rhs_now - apply_block(lblock, carried))
        return value, value

    start = jnp.zeros((STRAND_COUNT, B), jnp.float32)
    _, y_vals = lax.scan(forward, start, (dinv, lower, line_rhs, active))

    def backward(carried, items):
        dblock, ublock, y_now, act_now = items
        value = act_now[:, None] * (y_now - apply_block(dblock, apply_block(ublock, carried)))
        return value, value

    _, solution = lax.scan(backward, start, (dinv, upper, y_vals, active), reverse=True)
    return solution
```

```python
import functools

import jax
import jax.numpy as jnp
from jax import lax
from jax.experimental import pallas as pl
from jax.experimental.pallas import tpu as pltpu
from jax.sharding import PartitionSpec as P

MESH = pl.DeviceIdType.MESH
NT = (((1,), (1,)), ((), ()))
TN = (((0,), (0,)), ((), ()))
F32 = jnp.float32
BF = jnp.bfloat16
B = 162
TAIL = B - 128
CHUNK = 56
CODED = 168 + CHUNK
TOP = 32512.0


def dot(a, b):
    return jnp.dot(a, b, preferred_element_type=F32)


def halves(m):
    hi = m.astype(BF)
    return hi, (m - hi.astype(F32)).astype(BF)


def product(a, b):
    ah, al = halves(a)
    bh, bl = halves(b)
    return dot(ah, bh) + (dot(ah, bl) + dot(al, bh))


def two_rows(v):
    row = lax.broadcasted_iota(jnp.int32, v.shape, 0)
    hi = v.astype(BF).astype(F32)
    return jnp.where(row % 2 == 0, hi, v - hi).astype(BF)


def apply_map(matrix, v):
    out = lax.dot_general(two_rows(v), matrix, NT, preferred_element_type=F32)
    return out + pltpu.roll(out, 1, 0)


def wide(row):
    return jnp.broadcast_to(row, (8, B))


def kernel(
    state_ref, source_ref, coef_ref, nbr_ref, lift_ref, slot_ref, len_ref, d_hbm, l_hbm, u_hbm,
    out_ref,
    d_raw, l_raw, u_raw, wide_s, d_mat, l_mat, u_mat, ext, rhs, tail_s,
    send_a, recv_a, vec_a, got_vec_a, send_b, recv_b, vec_b, got_vec_b,
    map_h, map_l, y_s, c_out, c_in, e_out, e_in, x_out, x_in,
    load_sem, ext_ss, ext_rs, a_ss, a_rs, va_ss, va_rs, b_ss, b_rs, vb_ss, vb_rs,
    c_ss, c_rs, e_ss, e_rs, x_ss, x_rs,
):
    me = lax.axis_index("wall")
    surf = lax.axis_index("surf")
    wall_count = send_a.shape[0]
    lines = wall_count
    surf_count = lax.axis_size("surf")

    def dev(w):
        return (w, surf)

    loads = ((d_hbm, d_raw), (l_hbm, l_raw), (u_hbm, u_raw))

    def load(k, e, b):
        src, dst = loads[k]
        return pltpu.make_async_copy(
            src.at[e, :, pl.ds(pl.multiple_of(8 * b, 8), 8), :], dst.at[e, b], load_sem.at[k, e, b]
        )

    for b in range(4):
        for k in range(2):
            for e in range(2):
                load(k, e, b).start()
    for b in range(4):
        for e in range(2):
            load(2, e, b).start()

    barrier = pltpu.get_barrier_semaphore()
    after = lax.rem(surf + 1, surf_count)
    before = lax.rem(surf + surf_count - 1, surf_count)
    for s in (after, before):
        pl.semaphore_signal(barrier, inc=1, device_id=(me, s), device_id_type=MESH)

    @pl.loop(0, wall_count)
    def _(w):
        @pl.when(w != me)
        def _():
            pl.semaphore_signal(barrier, inc=1, device_id=dev(w), device_id_type=MESH)

    pl.semaphore_wait(barrier, wall_count - 1 + 2)

    halo = []
    for k, (s, place) in enumerate(((after, 0), (before, 2))):
        copy = pltpu.make_async_remote_copy(
            src_ref=state_ref, dst_ref=ext.at[place], send_sem=ext_ss.at[k], recv_sem=ext_rs.at[k],
            device_id=(me, s), device_id_type=MESH,
        )
        copy.start()
        halo.append(copy)
    ext[1] = state_ref[...]
    tail_s[...] = jnp.zeros_like(tail_s)

    kpos = lax.broadcasted_iota(jnp.int32, (192, 64), 0)
    own = kpos == 64 + lax.broadcasted_iota(jnp.int32, (192, 64), 1)
    weight = jnp.zeros((192, 64), F32)
    for f in range(4):
        hit = kpos == nbr_ref[pl.ds(f, 1), :]
        weight = weight + coef_ref[pl.ds(f, 1), :] * (own.astype(F32) - hit.astype(F32))
    for copy in halo:
        copy.wait()
    w1 = weight.astype(BF)
    rest = weight - w1.astype(F32)
    w2 = rest.astype(BF)
    w3 = (rest - w2.astype(F32)).astype(BF)
    cells = ext[...].reshape(192, B)
    face_sum = sum(
        lax.dot_general(w, cells, TN, preferred_element_type=F32) for w in (w3, w2, w1)
    ).astype(BF)
    spos = lax.broadcasted_iota(jnp.int32, (64, 32), 0)
    for e in range(2):
        pick = (spos == slot_ref[pl.ds(e, 1), :]).astype(F32).astype(BF)
        faces = lax.dot_general(pick, face_sum, TN, preferred_element_type=F32).astype(BF)
        mine = lax.dot_general(pick, source_ref[...], TN, preferred_element_type=F32)
        rhs[e] = mine - dot(faces, lift_ref[...])

    def active(e, l):
        return jnp.where(2 * me + e < len_ref[l], 1.0, 0.0).astype(F32)

    def widen(k, slot, e, b):
        raw = loads[k][1]

        @pl.loop(0, 9)
        def _(i):
            v = raw[e, b, pl.ds(i * 18, 18)].astype(F32)
            rows = pl.ds(pl.multiple_of(i * 144, 8), 144)
            wide_s[slot, 0, rows, :] = v[:, :, :128].reshape(144, 128)
            wide_s[slot, 1, rows, pl.ds(0, TAIL)] = v[:, :, 128:].reshape(144, TAIL)

    def one_line(slot, u, dst, e, l):
        dst[e, l, :, pl.ds(0, 128)] = wide_s[slot, 0, pl.ds(u, B, stride=8), :].astype(BF)
        high = wide_s[slot, 1, pl.ds(u, B, stride=8), :]
        dst[e, l, :, pl.ds(128, TAIL)] = high[:, :TAIL].astype(BF)

    def encode(m, store, vec, l, t):
        top = jnp.max(jnp.abs(m), axis=0, keepdims=True)
        inv = jnp.where(top > 0.0, TOP / jnp.where(top > 0.0, top, 1.0), 0.0)
        vec[l, pl.ds(1, 1), :] = top * (1.0 / TOP)
        q = jnp.floor(m * inv + 0.5)
        store[l, pl.ds(0, B), :] = q[:, :128].astype(jnp.int32).astype(jnp.int16)
        tail_s[t, pl.ds(0, B), pl.ds(0, TAIL)] = q[:, 128:]
        packed = tail_s[t, pl.ds(0, CHUNK), :]
        packed = packed + pltpu.roll(tail_s[t, pl.ds(CHUNK, CHUNK), :], 42, 1)
        packed = packed + pltpu.roll(tail_s[t, pl.ds(2 * CHUNK, CHUNK), :], 84, 1)
        store[l, pl.ds(168, CHUNK), :] = packed.astype(jnp.int32).astype(jnp.int16)

    def decode(coded, d, t):
        def split(q):
            v = q.astype(jnp.int32).astype(F32)
            hi = jnp.floor(v * (1.0 / 256.0) + 0.5)
            return hi, v - 256.0 * hi

        hi, lo = split(coded[d, pl.ds(0, B), :])
        map_h[d, :, pl.ds(0, 128)] = hi.astype(BF)
        map_l[d, :, pl.ds(0, 128)] = lo.astype(BF)
        packed = coded[d, pl.ds(168, CHUNK), :].astype(jnp.int32).astype(F32)
        for k, shift in ((0, 0), (1, 128 - 42), (2, 128 - 84)):
            part = packed if shift == 0 else pltpu.roll(packed, shift, 1)
            tail_s[t, pl.ds(k * CHUNK, CHUNK), pl.ds(0, TAIL)] = part[:, :TAIL]
        v = tail_s[t, pl.ds(0, B), :][:, :TAIL]
        hi = jnp.floor(v * (1.0 / 256.0) + 0.5)
        map_h[d, :, pl.ds(128, TAIL)] = hi.astype(BF)
        map_l[d, :, pl.ds(128, TAIL)] = (v - 256.0 * hi).astype(BF)

    def apply_coded(d, scale, v):
        rows = two_rows(v * scale)
        out = 256.0 * lax.dot_general(rows, map_h[d], NT, preferred_element_type=F32)
        out = out + lax.dot_general(rows, map_l[d], NT, preferred_element_type=F32)
        return out + pltpu.roll(out, 1, 0)

    def post(src, dst, ss, rs, to):
        return pltpu.make_async_remote_copy(
            src_ref=src.at[to], dst_ref=dst.at[me], send_sem=ss.at[to], recv_sem=rs.at[me],
            device_id=dev(to), device_id_type=MESH,
        )

    def arrive(src, dst, ss, rs, frm):
        pltpu.make_async_remote_copy(
            src_ref=src.at[frm], dst_ref=dst.at[frm], send_sem=ss.at[frm], recv_sem=rs.at[frm],
            device_id=dev(frm), device_id_type=MESH,
        ).wait_recv()

    def deliver(src, dst, ss, rs, to):
        @pl.when(to != me)
        def _():
            post(src, dst, ss, rs, to).start()

        @pl.when(to == me)
        def _():
            dst[me] = src[me]

    def expect(src, dst, ss, rs, frm):
        @pl.when(frm != me)
        def _():
            arrive(src, dst, ss, rs, frm)

    msg_a = (send_a, recv_a, a_ss, a_rs)
    msg_va = (vec_a, got_vec_a, va_ss, va_rs)
    msg_b = (send_b, recv_b, b_ss, b_rs)
    msg_vb = (vec_b, got_vec_b, vb_ss, vb_rs)
    msg_c = (c_out, c_in, c_ss, c_rs)
    msg_e = (e_out, e_in, e_ss, e_rs)
    msg_x = (x_out, x_in, x_ss, x_rs)

    @pl.loop(0, 4)
    def _(b):
        for k in range(2):
            for e in range(2):
                load(k, e, b).wait()
                widen(k, 2 * k + e, e, b)

        @pl.loop(0, 4)
        def _(half):
            for t in range(2):
                u = 2 * half + t
                l = 8 * b + u
                for e in range(2):
                    one_line(e, u, d_mat, e, l)
                    one_line(2 + e, u, l_mat, e, l)
                first = active(0, l) * dot(d_mat[0, l], l_mat[0, l])
                second = active(1, l) * dot(d_mat[1, l], l_mat[1, l])
                encode(product(second, first), send_a, vec_a, l, t)
                y = active(0, l) * apply_map(d_mat[0, l], wide(rhs[0, pl.ds(l, 1), :]))
                y = wide(rhs[1, pl.ds(l, 1), :]) - apply_map(l_mat[1, l], y)
                y = active(1, l) * apply_map(d_mat[1, l], y)
                vec_a[l, pl.ds(0, 1), :] = y[:1]
            for t in range(2):
                l = 8 * b + 2 * half + t
                deliver(*msg_a, l)
                deliver(*msg_va, l)

    @pl.loop(0, 4)
    def _(b):
        for e in range(2):
            load(2, e, b).wait()
            widen(2, e, e, b)

        @pl.loop(0, 4)
        def _(half):
            for t in range(2):
                u = 2 * half + t
                l = 8 * b + u
                for e in range(2):
                    one_line(e, u, u_mat, e, l)
                first = active(0, l) * dot(d_mat[0, l], u_mat[0, l])
                second = active(1, l) * dot(d_mat[1, l], u_mat[1, l])
                encode(product(first, second), send_b, vec_b, l, t)
                vec_b[l, pl.ds(0, 1), :] = jnp.zeros((1, B), F32)

    @pl.loop(0, wall_count // 2)
    def _(i):
        for t in range(2):
            expect(*msg_a, 2 * i + t)
            expect(*msg_va, 2 * i + t)
        for t in range(2):
            decode(recv_a, 2 * i + t, t)

    @pl.loop(0, wall_count)
    def _(l):
        deliver(*msg_b, l)
        deliver(*msg_vb, l)

    def fwd(d, v):
        c_out[d] = v[:1]
        deliver(*msg_c, d)
        got = got_vec_a[d]
        return apply_coded(d, wide(got[1:2]), v) + wide(got[0:1])

    lax.fori_loop(0, wall_count, fwd, jnp.zeros((8, B), F32))

    @pl.loop(0, lines // 4)
    def _(i):
        for t in range(4):
            expect(*msg_c, 4 * i + t)
        for t in range(4):
            l = 4 * i + t
            v = wide(rhs[0, pl.ds(l, 1), :]) - apply_map(l_mat[0, l], wide(c_in[l]))
            y1 = active(0, l) * apply_map(d_mat[0, l], v)
            v = wide(rhs[1, pl.ds(l, 1), :]) - apply_map(l_mat[1, l], y1)
            y2 = active(1, l) * apply_map(d_mat[1, l], v)
            y_s[0, l] = y1
            y_s[1, l] = y2
            e = y1 - active(0, l) * apply_map(d_mat[0, l], apply_map(u_mat[0, l], y2))
            e_out[l] = e[:1]
        for t in range(4):
            deliver(*msg_e, 4 * i + t)

    @pl.loop(0, wall_count // 2)
    def _(i):
        for t in range(2):
            expect(*msg_b, 2 * i + t)
            expect(*msg_vb, 2 * i + t)
        for t in range(2):
            decode(recv_b, 2 * i + t, t)

    def bwd(i, v):
        d = wall_count - 1 - i
        x_out[d] = v[:1]
        deliver(*msg_x, d)
        expect(*msg_e, d)
        got = got_vec_b[d]
        return apply_coded(d, wide(got[1:2]), v) + wide(e_in[d])

    lax.fori_loop(0, wall_count, bwd, jnp.zeros((8, B), F32))

    @pl.loop(0, lines // 4)
    def _(i):
        for t in range(4):
            expect(*msg_x, 4 * i + t)
        for t in range(4):
            l = 4 * i + t
            v = apply_map(d_mat[1, l], apply_map(u_mat[1, l], wide(x_in[l])))
            x2 = y_s[1, l] - active(1, l) * v
            v = apply_map(d_mat[0, l], apply_map(u_mat[0, l], x2))
            x1 = y_s[0, l] - active(0, l) * v
            out_ref[0, pl.ds(l, 1), :] = x1[:1]
            out_ref[1, pl.ds(l, 1), :] = x2[:1]

    @pl.loop(0, wall_count)
    def _(w):
        @pl.when(w != me)
        def _():
            for msg in (msg_a, msg_va, msg_b, msg_vb, msg_c, msg_e, msg_x):
                post(*msg, w).wait_send()


def per_device(state, source, face_coef, neighbour, lift, elem_slot, line_len, dinv, lower, upper):
    wall = lax.axis_size("wall")
    lines = dinv.shape[1]
    vmem = pl.BlockSpec(memory_space=pltpu.VMEM)
    hbm = pl.BlockSpec(memory_space=pl.ANY)
    raw = pltpu.VMEM((2, 4, B, 8, B), BF)
    mat = pltpu.VMEM((2, lines, B, B), BF)
    coded = pltpu.VMEM((wall, CODED, 128), jnp.int16)
    vec = pltpu.VMEM((wall, 2, B), F32)
    row = pltpu.VMEM((wall, 1, B), F32)
    sems = pltpu.SemaphoreType.DMA((wall,))
    turned = [jnp.transpose(m, (0, 2, 1, 3)) for m in (dinv, lower, upper)]
    return pl.pallas_call(
        kernel,
        out_shape=jax.ShapeDtypeStruct((2, lines, B), F32),
        in_specs=[vmem] * 6 + [pl.BlockSpec(memory_space=pltpu.SMEM)] + [hbm] * 3,
        out_specs=vmem,
        scratch_shapes=[
            raw, raw, raw,
            pltpu.VMEM((4, 2, 8 * B, 128), F32),
            mat, mat, mat,
            pltpu.VMEM((3, 64, B), BF),
            pltpu.VMEM((2, 32, B), F32),
            pltpu.VMEM((2, 168, 128), F32),
            coded, coded, vec, vec, coded, coded, vec, vec,
            pltpu.VMEM((wall, B, B), BF), pltpu.VMEM((wall, B, B), BF),
            pltpu.VMEM((2, lines, 8, B), F32),
            row, row, row, row, row, row,
            pltpu.SemaphoreType.DMA((3, 2, 4)),
            pltpu.SemaphoreType.DMA((2,)), pltpu.SemaphoreType.DMA((2,)),
        ] + [sems] * 14,
        compiler_params=pltpu.CompilerParams(
            collective_id=0, has_side_effects=True, vmem_limit_bytes=67043328
        ),
        name="lines",
    )(state, source, face_coef.T, neighbour.T, lift, elem_slot, line_len, *turned)


def solution(mesh):
    in_specs = (
        P(("wall", "surf"), None),
        P(("wall", "surf"), None),
        P(("wall", "surf"), None),
        P(("wall", "surf"), None),
        P(),
        P("wall", "surf"),
        P("surf"),
        P("wall", "surf", None, None),
        P("wall", "surf", None, None),
        P("wall", "surf", None, None),
    )
    return jax.shard_map(
        per_device, mesh=mesh, in_specs=in_specs, out_specs=P("wall", "surf", None), check_vma=False
    )
```

```python
import functools

import jax
import jax.numpy as jnp
from jax import lax
from jax.experimental import pallas as pl
from jax.experimental.pallas import tpu as pltpu
from jax.sharding import PartitionSpec as P

MESH = pl.DeviceIdType.MESH
NT = (((1,), (1,)), ((), ()))
TN = (((0,), (0,)), ((), ()))
F32 = jnp.float32
BF = jnp.bfloat16
B = 162
TAIL = B - 128
CHUNK = 56
EARLY = 2
CODED = 168 + CHUNK
TOP = 32512.0
ROUND = 12582912.0


def dot(a, b):
    return jnp.dot(a, b, preferred_element_type=F32)


def halves(m):
    hi = m.astype(BF)
    return hi, (m - hi.astype(F32)).astype(BF)


def product(a, b):
    ah, al = halves(a)
    bh, bl = halves(b)
    return dot(ah, bh) + (dot(ah, bl) + dot(al, bh))


def two_rows(v):
    row = lax.broadcasted_iota(jnp.int32, v.shape, 0)
    hi = v.astype(BF).astype(F32)
    return jnp.where(row % 2 == 0, hi, v - hi).astype(BF)


def apply_map(matrix, v):
    out = lax.dot_general(two_rows(v), matrix, NT, preferred_element_type=F32)
    return out + pltpu.roll(out, 1, 0)


def wide(row):
    return jnp.broadcast_to(row, (8, B))


def kernel(
    state_ref, source_ref, coef_ref, nbr_ref, lift_ref, slot_ref, len_ref, d_hbm, l_hbm, u_hbm,
    out_ref,
    raw, wide_s, d_mat, l_mat, u_mat, ext, rhs, tail_s,
    send_a, recv_a, vec_a, got_vec_a, send_b, recv_b, vec_b, got_vec_b,
    map_h, map_l, y_s, c_out, c_in, e_out, e_in, x_out, x_in,
    load_sem, ext_ss, ext_rs, a_ss, a_rs, va_ss, va_rs, b_ss, b_rs, vb_ss, vb_rs,
    c_ss, c_rs, e_ss, e_rs, x_ss, x_rs,
):
    me = lax.axis_index("wall")
    surf = lax.axis_index("surf")
    wall_count = send_a.shape[0]
    lines = wall_count
    surf_count = lax.axis_size("surf")

    def dev(w):
        return (w, surf)

    hbm = (d_hbm, l_hbm, u_hbm)

    def block(i):
        return lax.rem(i + me // 8, 4)

    def line(b, u):
        return 8 * b + lax.rem(u + me, 8)

    def turn(j):
        return lax.rem(j + me, wall_count)

    def load(k, e, b):
        return pltpu.make_async_copy(
            hbm[k].at[e, :, pl.ds(pl.multiple_of(8 * b, 8), 8), :], raw.at[k, e, b], load_sem.at[k, e, b]
        )

    for ks in ((0, 1), (2,)):
        for i in range(4):
            for k in ks:
                for e in range(2):
                    load(k, e, block(i)).start()

    barrier = pltpu.get_barrier_semaphore()
    after = lax.rem(surf + 1, surf_count)
    before = lax.rem(surf + surf_count - 1, surf_count)
    for s in (after, before):
        pl.semaphore_signal(barrier, inc=1, device_id=(me, s), device_id_type=MESH)

    @pl.loop(0, wall_count)
    def _(w):
        @pl.when(w != me)
        def _():
            pl.semaphore_signal(barrier, inc=1, device_id=dev(w), device_id_type=MESH)

    def active(e, l):
        return jnp.where(2 * me + e < len_ref[l], 1.0, 0.0).astype(F32)

    def widen(k, e, b, slot, first, count):
        v = raw[k, e, b, pl.ds(first, count)].astype(F32)
        rows = pl.ds(pl.multiple_of(first * 8, 8), count * 8)
        wide_s[slot, 0, rows, :] = v[:, :, :128].reshape(count * 8, 128)
        wide_s[slot, 1, rows, pl.ds(0, TAIL)] = v[:, :, 128:].reshape(count * 8, TAIL)

    def one_line(slot, u):
        low = wide_s[slot, 0, pl.ds(u, B, stride=8), :].astype(BF)
        high = wide_s[slot, 1, pl.ds(u, B, stride=8), :]
        return jnp.concatenate([low, high[:, :TAIL].astype(BF)], axis=1)

    def encode(m, keep, store, vec, l, t):
        top = jnp.max(jnp.abs(m), axis=0, keepdims=True)
        inv = jnp.where(top > 0.0, TOP / jnp.where(top > 0.0, top, 1.0), 0.0)
        vec[l, pl.ds(1, 1), :] = top * (keep * (1.0 / TOP))
        q = (m * inv + ROUND) - ROUND
        store[l, pl.ds(0, B), :] = q[:, :128].astype(jnp.int32).astype(jnp.int16)
        tail_s[t, pl.ds(0, B), pl.ds(0, TAIL)] = q[:, 128:]
        packed = tail_s[t, pl.ds(0, CHUNK), :]
        packed = packed + pltpu.roll(tail_s[t, pl.ds(CHUNK, CHUNK), :], 42, 1)
        packed = packed + pltpu.roll(tail_s[t, pl.ds(2 * CHUNK, CHUNK), :], 84, 1)
        store[l, pl.ds(168, CHUNK), :] = packed.astype(jnp.int32).astype(jnp.int16)

    def decode(coded, d, t):
        def split(q):
            v = q.astype(jnp.int32).astype(F32)
            hi = (v * (1.0 / 256.0) + ROUND) - ROUND
            return hi, v - 256.0 * hi

        hi, lo = split(coded[d, pl.ds(0, B), :])
        map_h[d, :, pl.ds(0, 128)] = hi.astype(BF)
        map_l[d, :, pl.ds(0, 128)] = lo.astype(BF)
        packed = coded[d, pl.ds(168, CHUNK), :].astype(jnp.int32).astype(F32)
        for k, shift in ((0, 0), (1, 128 - 42), (2, 128 - 84)):
            part = packed if shift == 0 else pltpu.roll(packed, shift, 1)
            tail_s[t, pl.ds(k * CHUNK, CHUNK), pl.ds(0, TAIL)] = part[:, :TAIL]
        v = tail_s[t, pl.ds(0, B), :][:, :TAIL]
        hi = (v * (1.0 / 256.0) + ROUND) - ROUND
        map_h[d, :, pl.ds(128, TAIL)] = hi.astype(BF)
        map_l[d, :, pl.ds(128, TAIL)] = (v - 256.0 * hi).astype(BF)

    def apply_coded(d, scale, v):
        rows = two_rows(v * scale)
        out = 256.0 * lax.dot_general(rows, map_h[d], NT, preferred_element_type=F32)
        out = out + lax.dot_general(rows, map_l[d], NT, preferred_element_type=F32)
        return out + pltpu.roll(out, 1, 0)

    def post(src, dst, ss, rs, to):
        return pltpu.make_async_remote_copy(
            src_ref=src.at[to], dst_ref=dst.at[me], send_sem=ss.at[to], recv_sem=rs.at[me],
            device_id=dev(to), device_id_type=MESH,
        )

    def arrive(src, dst, ss, rs, frm):
        pltpu.make_async_remote_copy(
            src_ref=src.at[frm], dst_ref=dst.at[frm], send_sem=ss.at[frm], recv_sem=rs.at[frm],
            device_id=dev(frm), device_id_type=MESH,
        ).wait_recv()

    def deliver(src, dst, ss, rs, to):
        @pl.when(to != me)
        def _():
            post(src, dst, ss, rs, to).start()

        @pl.when(to == me)
        def _():
            dst[me] = src[me]

    def expect(src, dst, ss, rs, frm):
        @pl.when(frm != me)
        def _():
            arrive(src, dst, ss, rs, frm)

    msg_a = (send_a, recv_a, a_ss, a_rs)
    msg_va = (vec_a, got_vec_a, va_ss, va_rs)
    msg_b = (send_b, recv_b, b_ss, b_rs)
    msg_vb = (vec_b, got_vec_b, vb_ss, vb_rs)
    msg_c = (c_out, c_in, c_ss, c_rs)
    msg_e = (e_out, e_in, e_ss, e_rs)
    msg_x = (x_out, x_in, x_ss, x_rs)

    tail_s[...] = jnp.zeros_like(tail_s)

    def widen_whole(ks, b, base):
        for n, k in enumerate(ks):
            for e in range(2):
                load(k, e, b).wait()

        @pl.loop(0, 6)
        def _(i):
            for n, k in enumerate(ks):
                for e in range(2):
                    widen(k, e, b, base + 2 * n + e, i * 27, 27)

    def fwd_maps(i, half, send):
        b, after_b = block(i), block(jnp.minimum(i + 1, 3))
        base, other = 4 * lax.rem(i, 2), 4 * lax.rem(i + 1, 2)
        ls = [line(b, 4 * half + t) for t in range(4)]
        for t, l in enumerate(ls):
            u = lax.rem(l, 8)
            m = [one_line(base + s, u) for s in range(4)]
            for e in range(2):
                d_mat[e, l] = m[e]
                l_mat[e, l] = m[2 + e]
            encode(product(dot(m[1], m[3]), dot(m[0], m[2])), active(1, l), send_a, vec_a, l, t)
        for n, k in enumerate((0, 1)):
            for e in range(2):
                widen(k, e, after_b, other + 2 * n + e, half * 81, 81)
        if send:
            for l in ls:
                deliver(*msg_a, l)

    def back_maps(i, half):
        b, after_b = block(i), block(jnp.minimum(i + 1, 3))
        base, other = 4 * lax.rem(i, 2), 4 * lax.rem(i + 1, 2)
        ls = [line(b, 4 * half + t) for t in range(4)]
        for t, l in enumerate(ls):
            u = lax.rem(l, 8)
            m = [one_line(base + s, u) for s in range(2)]
            for e in range(2):
                u_mat[e, l] = m[e]
            both = product(dot(d_mat[0, l], m[0]), dot(d_mat[1, l], m[1]))
            encode(both, active(1, l), send_b, vec_b, l, t)
            vec_b[l, pl.ds(0, 1), :] = jnp.zeros((1, B), F32)
        for e in range(2):
            widen(2, e, after_b, other + e, half * 81, 81)
        for l in ls:
            deliver(*msg_b, l)
            deliver(*msg_vb, l)

    def ready(ks, i):
        @pl.when(i < 3)
        def _():
            for k in ks:
                for e in range(2):
                    load(k, e, block(i + 1)).wait()

    widen_whole((0, 1), block(0), 0)
    ready((0, 1), 0)

    @pl.loop(0, 2)
    def _(half):
        fwd_maps(0, half, False)

    pl.semaphore_wait(barrier, wall_count - 1 + 2)
    halo = []
    for k, (s, place) in enumerate(((after, 0), (before, 2))):
        copy = pltpu.make_async_remote_copy(
            src_ref=state_ref, dst_ref=ext.at[place], send_sem=ext_ss.at[k], recv_sem=ext_rs.at[k],
            device_id=(me, s), device_id_type=MESH,
        )
        copy.start()
        halo.append(copy)
    ext[1] = state_ref[...]

    @pl.loop(0, 8)
    def _(u):
        deliver(*msg_a, line(block(0), u))

    @pl.loop(1, 4)
    def _(i):
        ready((0, 1), i)

        @pl.loop(0, 2)
        def _(half):
            fwd_maps(i, half, True)

    kpos = lax.broadcasted_iota(jnp.int32, (192, 64), 0)
    own = kpos == 64 + lax.broadcasted_iota(jnp.int32, (192, 64), 1)
    weight = jnp.zeros((192, 64), F32)
    for f in range(4):
        hit = kpos == nbr_ref[pl.ds(f, 1), :]
        weight = weight + coef_ref[pl.ds(f, 1), :] * (own.astype(F32) - hit.astype(F32))
    for copy in halo:
        copy.wait()
    w1 = weight.astype(BF)
    rest = weight - w1.astype(F32)
    w2 = rest.astype(BF)
    w3 = (rest - w2.astype(F32)).astype(BF)
    cells = ext[...].reshape(192, B)
    face_sum = sum(
        lax.dot_general(w, cells, TN, preferred_element_type=F32) for w in (w3, w2, w1)
    ).astype(BF)
    spos = lax.broadcasted_iota(jnp.int32, (64, 32), 0)
    for e in range(2):
        pick = (spos == slot_ref[pl.ds(e, 1), :]).astype(F32).astype(BF)
        faces = lax.dot_general(pick, face_sum, TN, preferred_element_type=F32).astype(BF)
        mine = lax.dot_general(pick, source_ref[...], TN, preferred_element_type=F32)
        rhs[e] = mine - dot(faces, lift_ref[...])

    @pl.loop(0, lines // 8)
    def _(i):
        for t in range(8):
            l = turn(8 * i + t)
            y = active(0, l) * apply_map(d_mat[0, l], wide(rhs[0, pl.ds(l, 1), :]))
            y = wide(rhs[1, pl.ds(l, 1), :]) - apply_map(l_mat[1, l], y)
            y = active(1, l) * apply_map(d_mat[1, l], y)
            vec_a[l, pl.ds(0, 1), :] = y[:1]
        for t in range(8):
            deliver(*msg_va, turn(8 * i + t))

    def back_range(lo, hi):
        @pl.loop(lo, hi)
        def _(i):
            ready((2,), i)

            @pl.loop(0, 2)
            def _(half):
                back_maps(i, half)

    widen_whole((2,), block(0), 0)
    back_range(0, EARLY)

    @pl.loop(0, wall_count // 2)
    def _(i):
        for t in range(2):
            expect(*msg_a, 2 * i + t)
            expect(*msg_va, 2 * i + t)
        for t in range(2):
            decode(recv_a, 2 * i + t, t)

    def fwd_step(d, v):
        got = got_vec_a[d]
        return apply_coded(d, wide(got[1:2]), v) + wide(got[0:1])

    def fwd(d, v):
        c_out[d] = v[:1]
        post(*msg_c, d).start()
        return fwd_step(d, v)

    v = lax.fori_loop(0, me, fwd, jnp.zeros((8, B), F32))
    c_in[me] = v[:1]
    lax.fori_loop(me + 1, wall_count, fwd, fwd_step(me, v))

    back_range(EARLY, 4)

    @pl.loop(0, lines // 8)
    def _(i):
        for t in range(8):
            expect(*msg_c, turn(8 * i + t))
        for t in range(8):
            l = turn(8 * i + t)
            v = wide(rhs[0, pl.ds(l, 1), :]) - apply_map(l_mat[0, l], wide(c_in[l]))
            y1 = active(0, l) * apply_map(d_mat[0, l], v)
            v = wide(rhs[1, pl.ds(l, 1), :]) - apply_map(l_mat[1, l], y1)
            y2 = active(1, l) * apply_map(d_mat[1, l], v)
            y_s[0, l] = y1
            y_s[1, l] = y2
            e = y1 - active(0, l) * apply_map(d_mat[0, l], apply_map(u_mat[0, l], y2))
            e_out[l] = e[:1]
        for t in range(8):
            deliver(*msg_e, turn(8 * i + t))

    @pl.loop(0, wall_count // 2)
    def _(i):
        for t in range(2):
            expect(*msg_b, 2 * i + t)
            expect(*msg_vb, 2 * i + t)
        for t in range(2):
            decode(recv_b, 2 * i + t, t)

    def bwd_step(d, v):
        got = got_vec_b[d]
        return apply_coded(d, wide(got[1:2]), v) + wide(e_in[d])

    def bwd(i, v):
        d = wall_count - 1 - i
        x_out[d] = v[:1]
        post(*msg_x, d).start()
        arrive(*msg_e, d)
        return bwd_step(d, v)

    last = wall_count - 1 - me
    v = lax.fori_loop(0, last, bwd, jnp.zeros((8, B), F32))
    x_in[me] = v[:1]
    lax.fori_loop(last + 1, wall_count, bwd, bwd_step(me, v))

    @pl.loop(0, lines // 8)
    def _(i):
        for t in range(8):
            expect(*msg_x, turn(8 * i + t))
        for t in range(8):
            l = turn(8 * i + t)
            v = apply_map(d_mat[1, l], apply_map(u_mat[1, l], wide(x_in[l])))
            x2 = y_s[1, l] - active(1, l) * v
            v = apply_map(d_mat[0, l], apply_map(u_mat[0, l], x2))
            x1 = y_s[0, l] - active(0, l) * v
            out_ref[0, pl.ds(l, 1), :] = x1[:1]
            out_ref[1, pl.ds(l, 1), :] = x2[:1]

    @pl.loop(0, wall_count)
    def _(w):
        @pl.when(w != me)
        def _():
            for msg in (msg_a, msg_va, msg_b, msg_vb, msg_c, msg_e, msg_x):
                post(*msg, w).wait_send()


def per_device(state, source, face_coef, neighbour, lift, elem_slot, line_len, dinv, lower, upper):
    wall = lax.axis_size("wall")
    lines = dinv.shape[1]
    vmem = pl.BlockSpec(memory_space=pltpu.VMEM)
    hbm = pl.BlockSpec(memory_space=pl.ANY)
    raw = pltpu.VMEM((3, 2, 4, B, 8, B), BF)
    mat = pltpu.VMEM((2, lines, B, B), BF)
    coded = pltpu.VMEM((wall, CODED, 128), jnp.int16)
    vec = pltpu.VMEM((wall, 2, B), F32)
    row = pltpu.VMEM((wall, 1, B), F32)
    sems = pltpu.SemaphoreType.DMA((wall,))
    turned = [jnp.transpose(m, (0, 2, 1, 3)) for m in (dinv, lower, upper)]
    return pl.pallas_call(
        kernel,
        out_shape=jax.ShapeDtypeStruct((2, lines, B), F32),
        in_specs=[vmem] * 6 + [pl.BlockSpec(memory_space=pltpu.SMEM)] + [hbm] * 3,
        out_specs=vmem,
        scratch_shapes=[
            raw,
            pltpu.VMEM((8, 2, 8 * B, 128), F32),
            mat, mat, mat,
            pltpu.VMEM((3, 64, B), BF),
            pltpu.VMEM((2, 32, B), F32),
            pltpu.VMEM((4, 168, 128), F32),
            coded, coded, vec, vec, coded, coded, vec, vec,
            pltpu.VMEM((wall, B, B), BF), pltpu.VMEM((wall, B, B), BF),
            pltpu.VMEM((2, lines, 8, B), F32),
            row, row, row, row, row, row,
            pltpu.SemaphoreType.DMA((3, 2, 4)),
            pltpu.SemaphoreType.DMA((2,)), pltpu.SemaphoreType.DMA((2,)),
        ] + [sems] * 14,
        compiler_params=pltpu.CompilerParams(
            collective_id=0, has_side_effects=True, vmem_limit_bytes=67043328
        ),
        name="lines",
    )(state, source, face_coef.T, neighbour.T, lift, elem_slot, line_len, *turned)


def solution(mesh):
    in_specs = (
        P(("wall", "surf"), None),
        P(("wall", "surf"), None),
        P(("wall", "surf"), None),
        P(("wall", "surf"), None),
        P(),
        P("wall", "surf"),
        P("surf"),
        P("wall", "surf", None, None),
        P("wall", "surf", None, None),
        P("wall", "surf", None, None),
    )
    return jax.shard_map(
        per_device, mesh=mesh, in_specs=in_specs, out_specs=P("wall", "surf", None), check_vma=False
    )
```

```python
import functools

import jax
import jax.numpy as jnp
from jax import lax
from jax.experimental import pallas as pl
from jax.experimental.pallas import tpu as pltpu
from jax.sharding import PartitionSpec as P

MESH = pl.DeviceIdType.MESH
NT = (((1,), (1,)), ((), ()))
TN = (((0,), (0,)), ((), ()))
F32 = jnp.float32
BF = jnp.bfloat16
B = 162
TAIL = B - 128
CHUNK = 56
FIRST = 8
CODED = 168 + CHUNK
TOP = 32512.0
ROUND = 12582912.0


def dot(a, b):
    return jnp.dot(a, b, preferred_element_type=F32)


def halves(m):
    hi = m.astype(BF)
    return hi, (m - hi.astype(F32)).astype(BF)


def product(a, b):
    ah, al = halves(a)
    bh, bl = halves(b)
    return dot(ah, bh) + (dot(ah, bl) + dot(al, bh))


def two_rows(v):
    row = lax.broadcasted_iota(jnp.int32, v.shape, 0)
    hi = v.astype(BF).astype(F32)
    return jnp.where(row % 2 == 0, hi, v - hi).astype(BF)


def apply_map(matrix, v):
    out = lax.dot_general(two_rows(v), matrix, NT, preferred_element_type=F32)
    return out + pltpu.roll(out, 1, 0)


def wide(row):
    return jnp.broadcast_to(row, (8, B))


def kernel(
    state_ref, source_ref, coef_ref, nbr_ref, lift_ref, slot_ref, len_ref, d_hbm, l_hbm, u_hbm,
    out_ref,
    raw, perm, last, prod, t_hi, t_lo, d_mat, l_mat, u_mat, ext, rhs, tail_s,
    send_a, recv_a, vec_a, got_vec_a, send_b, recv_b, vec_b, got_vec_b,
    map_h, map_l, y_s, c_out, c_in, e_out, e_in, x_out, x_in,
    load_sem, ext_ss, ext_rs, a_ss, a_rs, va_ss, va_rs, b_ss, b_rs, vb_ss, vb_rs,
    c_ss, c_rs, e_ss, e_rs, x_ss, x_rs,
):
    me = lax.axis_index("wall")
    surf = lax.axis_index("surf")
    wall_count = send_a.shape[0]
    lines = wall_count
    surf_count = lax.axis_size("surf")

    def dev(w):
        return (w, surf)

    hbm = (d_hbm, l_hbm, u_hbm)

    my_y, my_x, my_c = me // 8, lax.rem(me // 2, 4), lax.rem(me, 2)
    my_b, my_u = lax.rem(my_x + my_y, 4), 2 * my_y + my_c
    mine = 8 * my_b + my_u

    def block(i):
        return lax.rem(i + my_b, 4)

    def line(b, u):
        return 8 * b + lax.rem(u + my_u, 8)

    def owner(l):
        y = lax.rem(l, 8) // 2
        return 8 * y + 2 * lax.rem(l // 8 - y + 4, 4) + lax.rem(l, 2)

    def turn(j):
        return line(block(j // 8), lax.rem(j, 8))

    def away(j):
        return lax.rem(j + me, wall_count)

    def load(k, e, b):
        return pltpu.make_async_copy(
            hbm[k].at[e, :, pl.ds(pl.multiple_of(8 * b, 8), 8), :], raw.at[k, e, b], load_sem.at[k, e, b]
        )

    for ks in ((0, 1), (2,)):
        for i in range(4):
            for k in ks:
                for e in range(2):
                    load(k, e, block(i)).start()

    barrier = pltpu.get_barrier_semaphore()
    after = lax.rem(surf + 1, surf_count)
    before = lax.rem(surf + surf_count - 1, surf_count)
    for s in (after, before):
        pl.semaphore_signal(barrier, inc=1, device_id=(me, s), device_id_type=MESH)

    @pl.loop(0, wall_count)
    def _(w):
        @pl.when(w != me)
        def _():
            pl.semaphore_signal(barrier, inc=1, device_id=dev(w), device_id_type=MESH)

    def active(e, l):
        return jnp.where(2 * me + e < len_ref[l], 1.0, 0.0).astype(F32)

    def encode(m, keep, store, vec, l, t):
        top = jnp.max(jnp.abs(m), axis=0, keepdims=True)
        inv = jnp.where(top > 0.0, TOP / jnp.where(top > 0.0, top, 1.0), 0.0)
        vec[l, pl.ds(1, 1), :] = top * (keep * (1.0 / TOP))
        q = (m * inv + ROUND) - ROUND
        store[l, pl.ds(0, B), :] = q[:, :128].astype(jnp.int32).astype(jnp.int16)
        tail_s[t, pl.ds(0, B), pl.ds(0, TAIL)] = q[:, 128:]
        packed = tail_s[t, pl.ds(0, CHUNK), :]
        packed = packed + pltpu.roll(tail_s[t, pl.ds(CHUNK, CHUNK), :], 42, 1)
        packed = packed + pltpu.roll(tail_s[t, pl.ds(2 * CHUNK, CHUNK), :], 84, 1)
        store[l, pl.ds(168, CHUNK), :] = packed.astype(jnp.int32).astype(jnp.int16)

    def decode(coded, d, t):
        def split(q):
            v = q.astype(jnp.int32).astype(F32)
            hi = (v * (1.0 / 256.0) + ROUND) - ROUND
            return hi, v - 256.0 * hi

        hi, lo = split(coded[d, pl.ds(0, B), :])
        map_h[d, :, pl.ds(0, 128)] = hi.astype(BF)
        map_l[d, :, pl.ds(0, 128)] = lo.astype(BF)
        packed = coded[d, pl.ds(168, CHUNK), :].astype(jnp.int32).astype(F32)
        for k, shift in ((0, 0), (1, 128 - 42), (2, 128 - 84)):
            part = packed if shift == 0 else pltpu.roll(packed, shift, 1)
            tail_s[t, pl.ds(k * CHUNK, CHUNK), pl.ds(0, TAIL)] = part[:, :TAIL]
        v = tail_s[t, pl.ds(0, B), :][:, :TAIL]
        hi = (v * (1.0 / 256.0) + ROUND) - ROUND
        map_h[d, :, pl.ds(128, TAIL)] = hi.astype(BF)
        map_l[d, :, pl.ds(128, TAIL)] = (v - 256.0 * hi).astype(BF)

    def apply_coded(d, scale, v):
        rows = two_rows(v * scale)
        out = 256.0 * lax.dot_general(rows, map_h[d], NT, preferred_element_type=F32)
        out = out + lax.dot_general(rows, map_l[d], NT, preferred_element_type=F32)
        return out + pltpu.roll(out, 1, 0)

    def copy_of(src, dst, ss, rs, slot, place, to):
        return pltpu.make_async_remote_copy(
            src_ref=src.at[slot], dst_ref=dst.at[place], send_sem=ss,
            recv_sem=rs.at[place] if rs.shape else rs, device_id=dev(to), device_id_type=MESH,
        )

    def to_owner(msg, l):
        copy_of(*msg, l, me, owner(l)).start()

    def to_device(msg, d):
        copy_of(*msg, d, mine, d).start()

    def arrive(msg, frm):
        copy_of(*msg, frm, frm, frm).wait_recv()

    def everyone(src, dst, ss, rs):
        part = pl.ds(0, wall_count - 1)
        return pltpu.make_async_remote_copy(
            src_ref=src.at[part], dst_ref=dst.at[part], send_sem=ss,
            recv_sem=rs.at[0] if rs.shape else rs, device_id=dev(away(1)), device_id_type=MESH,
        )

    def send_turns(msg, lo, hi):
        @pl.loop(lo, hi)
        def _(j):
            to_owner(msg, turn(j))

    msg_a = (send_a, recv_a, a_ss, a_rs)
    msg_va = (vec_a, got_vec_a, va_ss, va_rs)
    msg_b = (send_b, recv_b, b_ss, b_rs)
    msg_vb = (vec_b, got_vec_b, vb_ss, vb_rs)
    msg_c = (c_out, c_in, c_ss, c_rs)
    msg_e = (e_out, e_in, e_ss, e_rs)
    msg_x = (x_out, x_in, x_ss, x_rs)

    tail_s[...] = jnp.zeros_like(tail_s)
    row = lax.broadcasted_iota(jnp.int32, (128, 128), 0)
    col = lax.broadcasted_iota(jnp.int32, (128, 128), 1)
    perm[...] = (col == 8 * lax.rem(row, 16) + row // 16).astype(F32).astype(BF)
    row = lax.broadcasted_iota(jnp.int32, (64, 16), 0)
    col = lax.broadcasted_iota(jnp.int32, (64, 16), 1)
    last[...] = (col == 8 * lax.rem(row, 8) + row // 8).astype(F32).astype(BF)

    def stored_product(t, a, b):
        return dot(t_hi[t, a], t_hi[t, b]) + (dot(t_hi[t, a], t_lo[t, b]) + dot(t_lo[t, a], t_hi[t, b]))

    def gather_lines(sources, b):
        for k, store in sources:
            for e in range(2):
                load(k, e, b).wait()

        @pl.loop(0, 2)
        def _(c):
            for t in range(5):
                first = pl.multiple_of(80 * c + 16 * t, 16)
                for k, store in sources:
                    for e in range(2):
                        x = raw[k, e, b, pl.ds(first, 16)].reshape(128, B)
                        y = dot(perm[...], x).astype(BF)
                        for u in range(8):
                            store[e, 8 * b + u, pl.ds(first, 16), :] = y[16 * u : 16 * u + 16]

        for k, store in sources:
            for e in range(2):
                x = raw[k, e, b, pl.ds(160, 2)].reshape(16, B)
                y = dot(last[...], x).astype(BF)
                for u in range(8):
                    store[e, 8 * b + u, pl.ds(160, 2), :] = y[8 * u : 8 * u + 2]

    def steps(b, right):
        for u in range(8):
            for e in range(2):
                t_hi[u, e], t_lo[u, e] = halves(dot(d_mat[e, 8 * b + u], right[e, 8 * b + u]))

    def fwd_maps(i, send):
        b = block(i)
        gather_lines(((0, d_mat), (1, l_mat)), b)
        steps(b, l_mat)

        for t in range(8):
            prod[t] = stored_product(t, 1, 0)
        for t in range(8):
            encode(prod[t], active(1, 8 * b + t), send_a, vec_a, 8 * b + t, t % 4)

        if send:
            @pl.loop(0, 8)
            def _(u):
                to_owner(msg_a, line(b, u))

    def back_maps(i):
        b = block(i)
        gather_lines(((2, u_mat),), b)
        steps(b, u_mat)

        for t in range(8):
            prod[t] = stored_product(t, 0, 1)
        for t in range(8):
            l = 8 * b + t
            encode(prod[t], active(1, l), send_b, vec_b, l, t % 4)
            vec_b[l, pl.ds(0, 1), :] = jnp.zeros((1, B), F32)

    fwd_maps(0, False)

    pl.semaphore_wait(barrier, wall_count - 1 + 2)
    halo = []
    for k, (s, place) in enumerate(((after, 0), (before, 2))):
        copy = pltpu.make_async_remote_copy(
            src_ref=state_ref, dst_ref=ext.at[place], send_sem=ext_ss.at[k], recv_sem=ext_rs.at[k],
            device_id=(me, s), device_id_type=MESH,
        )
        copy.start()
        halo.append(copy)
    ext[1] = state_ref[...]

    @pl.loop(1, 8)
    def _(u):
        to_owner(msg_a, line(block(0), u))

    recv_a[me] = send_a[mine]

    @pl.loop(1, 4)
    def _(i):
        fwd_maps(i, True)

    kpos = lax.broadcasted_iota(jnp.int32, (192, 64), 0)
    own = kpos == 64 + lax.broadcasted_iota(jnp.int32, (192, 64), 1)
    weight = jnp.zeros((192, 64), F32)
    for f in range(4):
        hit = kpos == nbr_ref[pl.ds(f, 1), :]
        weight = weight + coef_ref[pl.ds(f, 1), :] * (own.astype(F32) - hit.astype(F32))
    for copy in halo:
        copy.wait()
    w1 = weight.astype(BF)
    rest = weight - w1.astype(F32)
    w2 = rest.astype(BF)
    w3 = (rest - w2.astype(F32)).astype(BF)
    cells = ext[...].reshape(192, B)
    face_sum = sum(
        lax.dot_general(w, cells, TN, preferred_element_type=F32) for w in (w3, w2, w1)
    ).astype(BF)
    spos = lax.broadcasted_iota(jnp.int32, (64, 32), 0)
    for e in range(2):
        pick = (spos == slot_ref[pl.ds(e, 1), :]).astype(F32).astype(BF)
        faces = lax.dot_general(pick, face_sum, TN, preferred_element_type=F32).astype(BF)
        own_rows = lax.dot_general(pick, source_ref[...], TN, preferred_element_type=F32)
        rhs[e] = own_rows - dot(faces, lift_ref[...])

    @pl.loop(0, lines // 8)
    def _(i):
        ls = [turn(8 * i + t) for t in range(8)]
        y = [active(0, l) * apply_map(d_mat[0, l], wide(rhs[0, pl.ds(l, 1), :])) for l in ls]
        y = [wide(rhs[1, pl.ds(l, 1), :]) - apply_map(l_mat[1, l], v) for l, v in zip(ls, y)]
        y = [active(1, l) * apply_map(d_mat[1, l], v) for l, v in zip(ls, y)]
        for l, v in zip(ls, y):
            vec_a[l, pl.ds(0, 1), :] = v[:1]
        send_turns(msg_va, jnp.maximum(8 * i, 1), 8 * i + 8)

    got_vec_a[me] = vec_a[mine]

    def sender(j):
        return owner(8 * lax.rem(my_b - j // 8 + 4, 4) + lax.rem(my_u - j + 32, 8))

    def take(msg, i):
        @pl.loop(0, 4)
        def _(q):
            js = [8 * i + 2 * q + t for t in range(2)]
            for j in js:
                @pl.when(j > 0)
                def _():
                    arrive(msg, sender(j))
            for t, j in enumerate(js):
                decode(msg[1], sender(j), t)

    def send_back(lo, hi):
        @pl.loop(lo, hi)
        def _(j):
            to_owner(msg_b, turn(j))
            to_owner(msg_vb, turn(j))

    @pl.loop(0, 4)
    def _(i):
        back_maps(i)
        send_back(1, jnp.where(i == 0, FIRST, 1))
        take(msg_a, i)

    everyone(*msg_va).wait_recv()

    def send_four(msg, i):
        for t in range(4):
            @pl.when(4 * i + t != me)
            def _():
                to_device(msg, 4 * i + t)

    def fwd(i, v):
        for t in range(4):
            d = 4 * i + t
            c_out[d] = v[:1]
            got = got_vec_a[d]
            v = apply_coded(d, wide(got[1:2]), v) + wide(got[0:1])
        send_four(msg_c, i)
        return v

    lax.fori_loop(0, wall_count // 4, fwd, jnp.zeros((8, B), F32))
    c_in[mine] = c_out[me]

    send_back(FIRST, wall_count)

    everyone(*msg_c).wait_recv()

    @pl.loop(0, lines // 8)
    def _(i):
        ls = [turn(8 * i + t) for t in range(8)]
        v = [wide(rhs[0, pl.ds(l, 1), :]) - apply_map(l_mat[0, l], wide(c_in[l])) for l in ls]
        first = [active(0, l) * apply_map(d_mat[0, l], v) for l, v in zip(ls, v)]
        for l, y in zip(ls, first):
            y_s[0, l] = y
        v = [wide(rhs[1, pl.ds(l, 1), :]) - apply_map(l_mat[1, l], y) for l, y in zip(ls, first)]
        second = [active(1, l) * apply_map(d_mat[1, l], v) for l, v in zip(ls, v)]
        for l, y in zip(ls, second):
            y_s[1, l] = y
        v = [apply_map(u_mat[0, l], y) for l, y in zip(ls, second)]
        v = [active(0, l) * apply_map(d_mat[0, l], v) for l, v in zip(ls, v)]
        for l, y, e in zip(ls, first, v):
            e_out[l] = y[:1] - e[:1]
        send_turns(msg_e, jnp.maximum(8 * i, 1), 8 * i + 8)

    e_in[me] = e_out[mine]

    recv_b[me] = send_b[mine]
    got_vec_b[me] = vec_b[mine]

    @pl.loop(0, 4)
    def _(i):
        take(msg_b, i)

    everyone(*msg_vb).wait_recv()
    everyone(*msg_e).wait_recv()

    def bwd(k, v):
        i = wall_count // 4 - 1 - k
        for t in reversed(range(4)):
            d = 4 * i + t
            x_out[d] = v[:1]
            got = got_vec_b[d]
            v = apply_coded(d, wide(got[1:2]), v) + wide(e_in[d])
        send_four(msg_x, i)
        return v

    lax.fori_loop(0, wall_count // 4, bwd, jnp.zeros((8, B), F32))
    x_in[mine] = x_out[me]

    everyone(*msg_x).wait_recv()

    @pl.loop(0, lines // 8)
    def _(i):
        ls = [turn(8 * i + t) for t in range(8)]
        v = [apply_map(u_mat[1, l], wide(x_in[l])) for l in ls]
        v = [apply_map(d_mat[1, l], v) for l, v in zip(ls, v)]
        x = [y_s[1, l] - active(1, l) * v for l, v in zip(ls, v)]
        for l, v in zip(ls, x):
            out_ref[1, pl.ds(l, 1), :] = v[:1]
        v = [apply_map(u_mat[0, l], v) for l, v in zip(ls, x)]
        v = [apply_map(d_mat[0, l], v) for l, v in zip(ls, v)]
        for l, v in zip(ls, v):
            out_ref[0, pl.ds(l, 1), :] = y_s[0, l][:1] - active(0, l) * v[:1]

    for msg in (msg_a, msg_va, msg_b, msg_vb, msg_c, msg_e, msg_x):
        everyone(*msg).wait_send()


def per_device(state, source, face_coef, neighbour, lift, elem_slot, line_len, dinv, lower, upper):
    wall = lax.axis_size("wall")
    lines = dinv.shape[1]
    vmem = pl.BlockSpec(memory_space=pltpu.VMEM)
    hbm = pl.BlockSpec(memory_space=pl.ANY)
    raw = pltpu.VMEM((3, 2, 4, B, 8, B), BF)
    mat = pltpu.VMEM((2, lines, B, B), BF)
    coded = pltpu.VMEM((wall, CODED, 128), jnp.int16)
    vec = pltpu.VMEM((wall, 2, B), F32)
    row = pltpu.VMEM((wall, 1, B), F32)
    sems = pltpu.SemaphoreType.DMA((wall,))
    one = pltpu.SemaphoreType.DMA
    turned = [jnp.transpose(m, (0, 2, 1, 3)) for m in (dinv, lower, upper)]
    return pl.pallas_call(
        kernel,
        out_shape=jax.ShapeDtypeStruct((2, lines, B), F32),
        in_specs=[vmem] * 6 + [pl.BlockSpec(memory_space=pltpu.SMEM)] + [hbm] * 3,
        out_specs=vmem,
        scratch_shapes=[
            raw,
            pltpu.VMEM((128, 128), BF), pltpu.VMEM((64, 16), BF),
            pltpu.VMEM((8, B, B), F32),
            pltpu.VMEM((8, 2, B, B), BF), pltpu.VMEM((8, 2, B, B), BF),
            mat, mat, mat,
            pltpu.VMEM((3, 64, B), BF),
            pltpu.VMEM((2, 32, B), F32),
            pltpu.VMEM((4, 168, 128), F32),
            coded, coded, vec, vec, coded, coded, vec, vec,
            pltpu.VMEM((wall, B, B), BF), pltpu.VMEM((wall, B, B), BF),
            pltpu.VMEM((2, lines, 8, B), F32),
            row, row, row, row, row, row,
            pltpu.SemaphoreType.DMA((3, 2, 4)),
            pltpu.SemaphoreType.DMA((2,)), pltpu.SemaphoreType.DMA((2,)),
        ] + [one, sems, one, one, one, sems] + [one] * 8,
        compiler_params=pltpu.CompilerParams(
            collective_id=0, has_side_effects=True, vmem_limit_bytes=67043328
        ),
        name="lines",
    )(state, source, face_coef.T, neighbour.T, lift, elem_slot, line_len, *turned)


def solution(mesh):
    in_specs = (
        P(("wall", "surf"), None),
        P(("wall", "surf"), None),
        P(("wall", "surf"), None),
        P(("wall", "surf"), None),
        P(),
        P("wall", "surf"),
        P("surf"),
        P("wall", "surf", None, None),
        P("wall", "surf", None, None),
        P("wall", "surf", None, None),
    )
    return jax.shard_map(
        per_device, mesh=mesh, in_specs=in_specs, out_specs=P("wall", "surf", None), check_vma=False
    )
```

```python
import functools

import jax
import jax.numpy as jnp
from jax import lax
from jax.experimental import pallas as pl
from jax.experimental.pallas import tpu as pltpu
from jax.sharding import PartitionSpec as P

MESH = pl.DeviceIdType.MESH
NT = (((1,), (1,)), ((), ()))
TN = (((0,), (0,)), ((), ()))
F32 = jnp.float32
BF = jnp.bfloat16
B = 162
TAIL = B - 128
CHUNK = 56
FIRST = 16
CODED = 168 + CHUNK
TOP = 32512.0
ROUND = 12582912.0


def dot(a, b):
    return jnp.dot(a, b, preferred_element_type=F32)


def halves(m):
    hi = m.astype(BF)
    return hi, (m - hi.astype(F32)).astype(BF)


def product(a, b):
    ah, al = halves(a)
    bh, bl = halves(b)
    return dot(ah, bh) + (dot(ah, bl) + dot(al, bh))


def two_rows(v):
    row = lax.broadcasted_iota(jnp.int32, v.shape, 0)
    hi = v.astype(BF).astype(F32)
    return jnp.where(row % 2 == 0, hi, v - hi).astype(BF)


def apply_map(matrix, v):
    out = lax.dot_general(two_rows(v), matrix, NT, preferred_element_type=F32)
    return out + pltpu.roll(out, 1, 0)


def wide(row):
    return jnp.broadcast_to(row, (8, B))


def kernel(
    state_hbm, source_hbm, coef_hbm, nbr_hbm, lift_hbm, slot_hbm, len_ref, d_hbm, l_hbm, u_hbm,
    out_ref,
    source_ref, coef_ref, nbr_ref, lift_ref, slot_ref, v_mat, b_mat,
    raw, perm, last, prod, t_hi, t_lo, d_mat, l_mat, u_mat, ext, rhs, tail_s,
    send_a, recv_a, vec_a, got_vec_a, send_b, recv_b, vec_b, got_vec_b,
    map_h, map_l, y_s, c_out, c_in, e_out, e_in, x_out, x_in,
    small_sem, load_sem, ext_ss, ext_rs, a_ss, a_rs, va_ss, va_rs, b_ss, b_rs, vb_ss, vb_rs,
    c_ss, c_rs, e_ss, e_rs, x_ss, x_rs,
):
    me = lax.axis_index("wall")
    surf = lax.axis_index("surf")
    wall_count = send_a.shape[0]
    lines = wall_count
    surf_count = lax.axis_size("surf")

    def dev(w):
        return (w, surf)

    hbm = (d_hbm, l_hbm, u_hbm)

    my_y, my_x, my_c = me // 8, lax.rem(me // 2, 4), lax.rem(me, 2)
    my_b, my_u = lax.rem(my_x + my_y, 4), 2 * my_y + my_c
    mine = 8 * my_b + my_u

    def block(i):
        return lax.rem(i + my_b, 4)

    def line(b, u):
        return 8 * b + lax.rem(u + my_u, 8)

    def owner(l):
        y = lax.rem(l, 8) // 2
        return 8 * y + 2 * lax.rem(l // 8 - y + 4, 4) + lax.rem(l, 2)

    def turn(j):
        return line(block(j // 8), lax.rem(j, 8))

    def away(j):
        return lax.rem(j + me, wall_count)

    def load(k, e, b):
        return pltpu.make_async_copy(
            hbm[k].at[e, :, pl.ds(pl.multiple_of(8 * b, 8), 8), :], raw.at[k, e, b], load_sem.at[k, e, b]
        )

    for k in range(2):
        for e in range(2):
            load(k, e, block(0)).start()

    barrier = pltpu.get_barrier_semaphore()
    after = lax.rem(surf + 1, surf_count)
    before = lax.rem(surf + surf_count - 1, surf_count)
    for s in (after, before):
        pl.semaphore_signal(barrier, inc=1, device_id=(me, s), device_id_type=MESH)

    @pl.loop(0, wall_count)
    def _(w):
        @pl.when(w != me)
        def _():
            pl.semaphore_signal(barrier, inc=1, device_id=dev(w), device_id_type=MESH)

    def active(e, l):
        return jnp.where(2 * me + e < len_ref[l], 1.0, 0.0).astype(F32)

    def encode(m, keep, store, vec, l, t):
        top = jnp.maximum(jnp.max(jnp.abs(m), axis=0, keepdims=True), 1e-30)
        inv = TOP / top
        vec[l, pl.ds(1, 1), :] = top * (keep * (1.0 / TOP))
        q = (m * inv + ROUND) - ROUND
        store[l, pl.ds(0, B), :] = q[:, :128].astype(jnp.int32).astype(jnp.int16)
        tail_s[t, pl.ds(0, B), pl.ds(0, TAIL)] = q[:, 128:]
        packed = tail_s[t, pl.ds(0, CHUNK), :]
        packed = packed + pltpu.roll(tail_s[t, pl.ds(CHUNK, CHUNK), :], 42, 1)
        packed = packed + pltpu.roll(tail_s[t, pl.ds(2 * CHUNK, CHUNK), :], 84, 1)
        store[l, pl.ds(168, CHUNK), :] = packed.astype(jnp.int32).astype(jnp.int16)

    def decode(coded, d, t):
        def split(q):
            v = q.astype(jnp.int32).astype(F32)
            hi = (v * (1.0 / 256.0) + ROUND) - ROUND
            return hi, v - 256.0 * hi

        hi, lo = split(coded[d, pl.ds(0, B), :])
        map_h[d, :, pl.ds(0, 128)] = hi.astype(BF)
        map_l[d, :, pl.ds(0, 128)] = lo.astype(BF)
        packed = coded[d, pl.ds(168, CHUNK), :].astype(jnp.int32).astype(F32)
        for k, shift in ((0, 0), (1, 128 - 42), (2, 128 - 84)):
            part = packed if shift == 0 else pltpu.roll(packed, shift, 1)
            tail_s[t, pl.ds(k * CHUNK, CHUNK), pl.ds(0, TAIL)] = part[:, :TAIL]
        v = tail_s[t, pl.ds(0, B), :][:, :TAIL]
        hi = (v * (1.0 / 256.0) + ROUND) - ROUND
        map_h[d, :, pl.ds(128, TAIL)] = hi.astype(BF)
        map_l[d, :, pl.ds(128, TAIL)] = (v - 256.0 * hi).astype(BF)

    def apply_coded(d, scale, v):
        rows = two_rows(v * scale)
        out = 256.0 * lax.dot_general(rows, map_h[d], NT, preferred_element_type=F32)
        out = out + lax.dot_general(rows, map_l[d], NT, preferred_element_type=F32)
        return out + pltpu.roll(out, 1, 0)

    def copy_of(src, dst, ss, rs, slot, place, to):
        return pltpu.make_async_remote_copy(
            src_ref=src.at[slot], dst_ref=dst.at[place], send_sem=ss,
            recv_sem=rs.at[place] if rs.shape else rs, device_id=dev(to), device_id_type=MESH,
        )

    def to_owner(msg, l):
        copy_of(*msg, l, me, owner(l)).start()

    def to_device(msg, d):
        copy_of(*msg, d, mine, d).start()

    def arrive(msg, frm):
        copy_of(*msg, frm, frm, frm).wait_recv()

    def everyone(src, dst, ss, rs):
        part = pl.ds(0, wall_count - 1)
        return pltpu.make_async_remote_copy(
            src_ref=src.at[part], dst_ref=dst.at[part], send_sem=ss,
            recv_sem=rs.at[0] if rs.shape else rs, device_id=dev(away(1)), device_id_type=MESH,
        )

    def send_turns(msg, lo, hi):
        @pl.loop(lo, hi)
        def _(j):
            to_owner(msg, turn(j))

    msg_a = (send_a, recv_a, a_ss, a_rs)
    msg_va = (vec_a, got_vec_a, va_ss, va_rs)
    msg_b = (send_b, recv_b, b_ss, b_rs)
    msg_vb = (vec_b, got_vec_b, vb_ss, vb_rs)
    msg_c = (c_out, c_in, c_ss, c_rs)
    msg_e = (e_out, e_in, e_ss, e_rs)
    msg_x = (x_out, x_in, x_ss, x_rs)

    small = [
        pltpu.make_async_copy(src, dst, small_sem.at[n])
        for n, (src, dst) in enumerate((
            (state_hbm, ext.at[1]), (source_hbm, source_ref), (coef_hbm, coef_ref),
            (nbr_hbm, nbr_ref), (lift_hbm, lift_ref), (slot_hbm, slot_ref),
        ))
    ]
    for copy in small:
        copy.start()
    for ks, first in (((0, 1), 1), ((2,), 0)):
        for n in range(first, 4):
            for k in ks:
                for e in range(2):
                    load(k, e, block(n)).start()

    tail_s[...] = jnp.zeros_like(tail_s)
    row = lax.broadcasted_iota(jnp.int32, (128, 128), 0)
    col = lax.broadcasted_iota(jnp.int32, (128, 128), 1)
    perm[...] = (col == 8 * lax.rem(row, 16) + row // 16).astype(F32).astype(BF)
    row = lax.broadcasted_iota(jnp.int32, (64, 16), 0)
    col = lax.broadcasted_iota(jnp.int32, (64, 16), 1)
    last[...] = (col == 8 * lax.rem(row, 8) + row // 8).astype(F32).astype(BF)

    def stored_product(t, a, b):
        return dot(t_hi[t, a], t_hi[t, b]) + (dot(t_hi[t, a], t_lo[t, b]) + dot(t_lo[t, a], t_hi[t, b]))

    def gather_lines(sources, b):
        for k, store in sources:
            for e in range(2):
                load(k, e, b).wait()

        @pl.loop(0, 2)
        def _(c):
            for t in range(5):
                first = pl.multiple_of(80 * c + 16 * t, 16)
                for k, store in sources:
                    for e in range(2):
                        x = raw[k, e, b, pl.ds(first, 16)].reshape(128, B)
                        y = dot(perm[...], x).astype(BF)
                        for u in range(8):
                            store[e, 8 * b + u, pl.ds(first, 16), :] = y[16 * u : 16 * u + 16]

        for k, store in sources:
            for e in range(2):
                x = raw[k, e, b, pl.ds(160, 2)].reshape(16, B)
                y = dot(last[...], x).astype(BF)
                for u in range(8):
                    store[e, 8 * b + u, pl.ds(160, 2), :] = y[8 * u : 8 * u + 2]

    def steps(b, right):
        for u in range(8):
            for e in range(2):
                t_hi[u, e], t_lo[u, e] = halves(dot(d_mat[e, 8 * b + u], right[e, 8 * b + u]))

    def fwd_maps(i, send):
        b = block(i)
        gather_lines(((0, d_mat), (1, l_mat)), b)
        steps(b, l_mat)

        for t in range(8):
            prod[t] = stored_product(t, 1, 0)
        for t in range(8):
            encode(prod[t], active(1, 8 * b + t), send_a, vec_a, 8 * b + t, t % 4)

        if send:
            @pl.loop(0, 8)
            def _(u):
                to_owner(msg_a, line(b, u))

    def back_maps(i):
        b = block(i)
        gather_lines(((2, u_mat),), b)
        steps(b, u_mat)

        for t in range(8):
            prod[t] = stored_product(t, 0, 1)
        for t in range(8):
            l = 8 * b + t
            v_mat[l] = t_hi[t, 1]
            b_mat[l] = prod[t].astype(BF)
            encode(prod[t], active(1, l), send_b, vec_b, l, t % 4)
            vec_b[l, pl.ds(0, 1), :] = jnp.zeros((1, B), F32)

    fwd_maps(0, False)

    for copy in small:
        copy.wait()
    pl.semaphore_wait(barrier, wall_count - 1 + 2)
    halo = []
    for k, (s, place) in enumerate(((after, 0), (before, 2))):
        copy = pltpu.make_async_remote_copy(
            src_ref=ext.at[1], dst_ref=ext.at[place], send_sem=ext_ss.at[k], recv_sem=ext_rs.at[k],
            device_id=(me, s), device_id_type=MESH,
        )
        copy.start()
        halo.append(copy)

    @pl.loop(1, 8)
    def _(u):
        to_owner(msg_a, line(block(0), u))

    recv_a[me] = send_a[mine]

    @pl.loop(1, 4)
    def _(i):
        fwd_maps(i, True)

    kpos = lax.broadcasted_iota(jnp.int32, (192, 64), 0)
    own = kpos == 64 + lax.broadcasted_iota(jnp.int32, (192, 64), 1)
    weight = jnp.zeros((192, 64), F32)
    for f in range(4):
        hit = kpos == nbr_ref[pl.ds(f, 1), :]
        weight = weight + coef_ref[pl.ds(f, 1), :] * (own.astype(F32) - hit.astype(F32))
    for copy in halo:
        copy.wait()
    w1 = weight.astype(BF)
    rest = weight - w1.astype(F32)
    w2 = rest.astype(BF)
    w3 = (rest - w2.astype(F32)).astype(BF)
    cells = ext[...].reshape(192, B)
    face_sum = sum(
        lax.dot_general(w, cells, TN, preferred_element_type=F32) for w in (w3, w2, w1)
    ).astype(BF)
    spos = lax.broadcasted_iota(jnp.int32, (64, 32), 0)
    for e in range(2):
        pick = (spos == slot_ref[pl.ds(e, 1), :]).astype(F32).astype(BF)
        faces = lax.dot_general(pick, face_sum, TN, preferred_element_type=F32).astype(BF)
        own_rows = lax.dot_general(pick, source_ref[...], TN, preferred_element_type=F32)
        rhs[e] = own_rows - dot(faces, lift_ref[...])

    @pl.loop(0, lines // 8)
    def _(i):
        ls = [turn(8 * i + t) for t in range(8)]
        y = [active(0, l) * apply_map(d_mat[0, l], wide(rhs[0, pl.ds(l, 1), :])) for l in ls]
        y = [wide(rhs[1, pl.ds(l, 1), :]) - apply_map(l_mat[1, l], v) for l, v in zip(ls, y)]
        y = [active(1, l) * apply_map(d_mat[1, l], v) for l, v in zip(ls, y)]
        for l, v in zip(ls, y):
            vec_a[l, pl.ds(0, 1), :] = v[:1]
        send_turns(msg_va, jnp.maximum(8 * i, 1), 8 * i + 8)

    got_vec_a[me] = vec_a[mine]

    def sender(j):
        return owner(8 * lax.rem(my_b - j // 8 + 4, 4) + lax.rem(my_u - j + 32, 8))

    def take(msg, i):
        @pl.loop(0, 4)
        def _(q):
            js = [8 * i + 2 * q + t for t in range(2)]
            for j in js:
                @pl.when(j > 0)
                def _():
                    arrive(msg, sender(j))
            for t, j in enumerate(js):
                decode(msg[1], sender(j), t)

    def send_back(lo, hi):
        @pl.loop(lo, hi)
        def _(j):
            to_owner(msg_b, turn(j))
            to_owner(msg_vb, turn(j))

    @pl.loop(0, 4)
    def _(i):
        back_maps(i)
        send_back(jnp.maximum(8 * i, 1), jnp.minimum(8 * i + 8, FIRST))
        take(msg_a, i)

    everyone(*msg_va).wait_recv()

    def send_four(msg, i):
        for t in range(4):
            @pl.when(4 * i + t != me)
            def _():
                to_device(msg, 4 * i + t)

    def fwd(i, v):
        for t in range(4):
            d = 4 * i + t
            c_out[d] = v[:1]
            got = got_vec_a[d]
            v = apply_coded(d, wide(got[1:2]), v) + wide(got[0:1])
        send_four(msg_c, i)
        return v

    lax.fori_loop(0, wall_count // 4, fwd, jnp.zeros((8, B), F32))
    c_in[mine] = c_out[me]

    send_back(FIRST, wall_count)

    everyone(*msg_c).wait_recv()

    @pl.loop(0, lines // 8)
    def _(i):
        ls = [turn(8 * i + t) for t in range(8)]
        v = [wide(rhs[0, pl.ds(l, 1), :]) - apply_map(l_mat[0, l], wide(c_in[l])) for l in ls]
        first = [active(0, l) * apply_map(d_mat[0, l], v) for l, v in zip(ls, v)]
        v = [wide(rhs[1, pl.ds(l, 1), :]) - apply_map(l_mat[1, l], y) for l, y in zip(ls, first)]
        second = [active(1, l) * apply_map(d_mat[1, l], v) for l, v in zip(ls, v)]
        for l, y in zip(ls, second):
            y_s[1, l] = y
        v = [apply_map(u_mat[0, l], y) for l, y in zip(ls, second)]
        v = [active(0, l) * apply_map(d_mat[0, l], v) for l, v in zip(ls, v)]
        for l, y, e in zip(ls, first, v):
            e_out[l] = y[:1] - e[:1]
        send_turns(msg_e, jnp.maximum(8 * i, 1), 8 * i + 8)

    e_in[me] = e_out[mine]

    recv_b[me] = send_b[mine]
    got_vec_b[me] = vec_b[mine]

    @pl.loop(0, 4)
    def _(i):
        take(msg_b, i)

    everyone(*msg_vb).wait_recv()
    everyone(*msg_e).wait_recv()

    def bwd(k, v):
        i = wall_count // 4 - 1 - k
        for t in reversed(range(4)):
            d = 4 * i + t
            x_out[d] = v[:1]
            got = got_vec_b[d]
            v = apply_coded(d, wide(got[1:2]), v) + wide(e_in[d])
        send_four(msg_x, i)
        return v

    lax.fori_loop(0, wall_count // 4, bwd, jnp.zeros((8, B), F32))
    x_in[mine] = x_out[me]

    everyone(*msg_x).wait_recv()

    @pl.loop(0, lines // 8)
    def _(i):
        ls = [turn(8 * i + t) for t in range(8)]
        v = [apply_map(v_mat[l], wide(x_in[l])) for l in ls]
        w = [apply_map(b_mat[l], wide(x_in[l])) for l in ls]
        for l, v, w in zip(ls, v, w):
            out_ref[1, pl.ds(l, 1), :] = y_s[1, l][:1] - active(1, l) * v[:1]
            out_ref[0, pl.ds(l, 1), :] = e_out[l] + active(1, l) * w[:1]

    for msg in (msg_a, msg_va, msg_b, msg_vb, msg_c, msg_e, msg_x):
        everyone(*msg).wait_send()


def per_device(state, source, face_coef, neighbour, lift, elem_slot, line_len, dinv, lower, upper):
    wall = lax.axis_size("wall")
    lines = dinv.shape[1]
    vmem = pl.BlockSpec(memory_space=pltpu.VMEM)
    hbm = pl.BlockSpec(memory_space=pl.ANY)
    raw = pltpu.VMEM((3, 2, 4, B, 8, B), BF)
    mat = pltpu.VMEM((2, lines, B, B), BF)
    coded = pltpu.VMEM((wall, CODED, 128), jnp.int16)
    vec = pltpu.VMEM((wall, 2, B), F32)
    row = pltpu.VMEM((wall, 1, B), F32)
    sems = pltpu.SemaphoreType.DMA((wall,))
    one = pltpu.SemaphoreType.DMA
    turned = [jnp.transpose(m, (0, 2, 1, 3)) for m in (dinv, lower, upper)]
    return pl.pallas_call(
        kernel,
        out_shape=jax.ShapeDtypeStruct((2, lines, B), F32),
        in_specs=[hbm] * 6 + [pl.BlockSpec(memory_space=pltpu.SMEM)] + [hbm] * 3,
        out_specs=vmem,
        scratch_shapes=[
            pltpu.VMEM((64, B), BF), pltpu.VMEM((4, 64), F32), pltpu.VMEM((4, 64), jnp.int32),
            pltpu.VMEM((B, B), BF), pltpu.VMEM((2, lines), jnp.int32),
            pltpu.VMEM((lines, B, B), BF), pltpu.VMEM((lines, B, B), BF),
            raw,
            pltpu.VMEM((128, 128), BF), pltpu.VMEM((64, 16), BF),
            pltpu.VMEM((8, B, B), F32),
            pltpu.VMEM((8, 2, B, B), BF), pltpu.VMEM((8, 2, B, B), BF),
            mat, mat, mat,
            pltpu.VMEM((3, 64, B), BF),
            pltpu.VMEM((2, 32, B), F32),
            pltpu.VMEM((4, 168, 128), F32),
            coded, coded, vec, vec, coded, coded, vec, vec,
            pltpu.VMEM((wall, B, B), BF), pltpu.VMEM((wall, B, B), BF),
            pltpu.VMEM((2, lines, 8, B), F32),
            row, row, row, row, row, row,
            pltpu.SemaphoreType.DMA((6,)),
            pltpu.SemaphoreType.DMA((3, 2, 4)),
            pltpu.SemaphoreType.DMA((2,)), pltpu.SemaphoreType.DMA((2,)),
        ] + [one, sems, one, one, one, sems] + [one] * 8,
        compiler_params=pltpu.CompilerParams(
            collective_id=0, has_side_effects=True, vmem_limit_bytes=67043328
        ),
        name="lines",
    )(state, source, face_coef.T, neighbour.T, lift, elem_slot, line_len, *turned)


def solution(mesh):
    in_specs = (
        P(("wall", "surf"), None),
        P(("wall", "surf"), None),
        P(("wall", "surf"), None),
        P(("wall", "surf"), None),
        P(),
        P("wall", "surf"),
        P("surf"),
        P("wall", "surf", None, None),
        P("wall", "surf", None, None),
        P("wall", "surf", None, None),
    )
    return jax.shard_map(
        per_device, mesh=mesh, in_specs=in_specs, out_specs=P("wall", "surf", None), check_vma=False
    )
```

```python
import functools

import jax
import jax.numpy as jnp
from jax import lax
from jax.experimental import pallas as pl
from jax.experimental.pallas import tpu as pltpu
from jax.sharding import PartitionSpec as P

MESH = pl.DeviceIdType.MESH
NT = (((1,), (1,)), ((), ()))
TN = (((0,), (0,)), ((), ()))
F32 = jnp.float32
BF = jnp.bfloat16
B = 162
TAIL = B - 128
CHUNK = 56
FIRST = 16
CODED = 168 + CHUNK
TOP = 32512.0
ROUND = 12582912.0


def dot(a, b):
    return jnp.dot(a, b, preferred_element_type=F32)


def halves(m):
    hi = m.astype(BF)
    return hi, (m - hi.astype(F32)).astype(BF)


def product(a, b):
    ah, al = halves(a)
    bh, bl = halves(b)
    return dot(ah, bh) + (dot(ah, bl) + dot(al, bh))


def two_rows(v):
    row = lax.broadcasted_iota(jnp.int32, v.shape, 0)
    hi = v.astype(BF).astype(F32)
    return jnp.where(row % 2 == 0, hi, v - hi).astype(BF)


def apply_map(matrix, v):
    out = lax.dot_general(two_rows(v), matrix, NT, preferred_element_type=F32)
    return out + pltpu.roll(out, 1, 0)


def wide(row):
    return jnp.broadcast_to(row, (8, B))


def kernel(
    state_hbm, source_hbm, coef_hbm, nbr_hbm, lift_hbm, slot_hbm, len_ref, d_hbm, l_hbm, u_hbm,
    out_ref,
    source_ref, coef_ref, nbr_ref, lift_ref, slot_ref, v_mat, b_mat,
    raw, perm, last, prod, t_hi, t_lo, d_mat, l_mat, u_mat, ext, rhs, tail_s,
    send_a, recv_a, vec_a, got_vec_a, send_b, recv_b, vec_b, got_vec_b,
    map_h, map_l, y_s, c_out, c_in, e_out, e_in, x_out, x_in,
    small_sem, load_sem, ext_ss, ext_rs, a_ss, a_rs, va_ss, va_rs, b_ss, b_rs, vb_ss, vb_rs,
    c_ss, c_rs, e_ss, e_rs, x_ss, x_rs,
):
    me = lax.axis_index("wall")
    surf = lax.axis_index("surf")
    wall_count = send_a.shape[0]
    lines = wall_count
    surf_count = lax.axis_size("surf")

    def dev(w):
        return (w, surf)

    hbm = (d_hbm, l_hbm, u_hbm)

    my_y, my_x, my_c = me // 8, lax.rem(me // 2, 4), lax.rem(me, 2)
    my_b, my_u = lax.rem(my_x + my_y, 4), 2 * my_y + my_c
    mine = 8 * my_b + my_u

    def block(i):
        return lax.rem(i + my_b, 4)

    def line(b, u):
        return 8 * b + lax.rem(u + my_u, 8)

    def owner(l):
        y = lax.rem(l, 8) // 2
        return 8 * y + 2 * lax.rem(l // 8 - y + 4, 4) + lax.rem(l, 2)

    def turn(j):
        return line(block(j // 8), lax.rem(j, 8))

    def away(j):
        return lax.rem(j + me, wall_count)

    def load(k, e, b):
        return pltpu.make_async_copy(
            hbm[k].at[e, :, pl.ds(pl.multiple_of(8 * b, 8), 8), :], raw.at[k, e, b], load_sem.at[k, e, b]
        )

    for k in range(2):
        for e in range(2):
            load(k, e, block(0)).start()

    barrier = pltpu.get_barrier_semaphore()
    after = lax.rem(surf + 1, surf_count)
    before = lax.rem(surf + surf_count - 1, surf_count)
    for s in (after, before):
        pl.semaphore_signal(barrier, inc=1, device_id=(me, s), device_id_type=MESH)

    @pl.loop(0, wall_count)
    def _(w):
        @pl.when(w != me)
        def _():
            pl.semaphore_signal(barrier, inc=1, device_id=dev(w), device_id_type=MESH)

    def active(e, l):
        return jnp.where(2 * me + e < len_ref[l], 1.0, 0.0).astype(F32)

    def encode(m, keep, store, vec, l, t):
        top = jnp.maximum(jnp.max(jnp.abs(m), axis=0, keepdims=True), 1e-30)
        inv = TOP / top
        vec[l, pl.ds(1, 1), :] = top * (keep * (1.0 / TOP))
        q = (m * inv + ROUND) - ROUND
        store[l, pl.ds(0, B), :] = q[:, :128].astype(jnp.int32).astype(jnp.int16)
        tail_s[t, pl.ds(0, B), pl.ds(0, TAIL)] = q[:, 128:]
        packed = tail_s[t, pl.ds(0, CHUNK), :]
        packed = packed + pltpu.roll(tail_s[t, pl.ds(CHUNK, CHUNK), :], 42, 1)
        packed = packed + pltpu.roll(tail_s[t, pl.ds(2 * CHUNK, CHUNK), :], 84, 1)
        store[l, pl.ds(168, CHUNK), :] = packed.astype(jnp.int32).astype(jnp.int16)

    def decode(coded, d, t):
        def split(q):
            v = q.astype(jnp.int32).astype(F32)
            hi = (v * (1.0 / 256.0) + ROUND) - ROUND
            return hi, v - 256.0 * hi

        hi, lo = split(coded[d, pl.ds(0, B), :])
        map_h[d, :, pl.ds(0, 128)] = hi.astype(BF)
        map_l[d, :, pl.ds(0, 128)] = lo.astype(BF)
        packed = coded[d, pl.ds(168, CHUNK), :].astype(jnp.int32).astype(F32)
        for k, shift in ((0, 0), (1, 128 - 42), (2, 128 - 84)):
            part = packed if shift == 0 else pltpu.roll(packed, shift, 1)
            tail_s[t, pl.ds(k * CHUNK, CHUNK), pl.ds(0, TAIL)] = part[:, :TAIL]
        v = tail_s[t, pl.ds(0, B), :][:, :TAIL]
        hi = (v * (1.0 / 256.0) + ROUND) - ROUND
        map_h[d, :, pl.ds(128, TAIL)] = hi.astype(BF)
        map_l[d, :, pl.ds(128, TAIL)] = (v - 256.0 * hi).astype(BF)

    def apply_coded(d, scale, v):
        rows = two_rows(v * scale)
        out = 256.0 * lax.dot_general(rows, map_h[d], NT, preferred_element_type=F32)
        out = out + lax.dot_general(rows, map_l[d], NT, preferred_element_type=F32)
        return out + pltpu.roll(out, 1, 0)

    def copy_of(src, dst, ss, rs, slot, place, to):
        return pltpu.make_async_remote_copy(
            src_ref=src.at[slot], dst_ref=dst.at[place], send_sem=ss,
            recv_sem=rs.at[place] if rs.shape else rs, device_id=dev(to), device_id_type=MESH,
        )

    def to_owner(msg, l):
        copy_of(*msg, l, me, owner(l)).start()

    def to_device(msg, d):
        copy_of(*msg, d, mine, d).start()

    def arrive(msg, frm):
        copy_of(*msg, frm, frm, frm).wait_recv()

    def everyone(src, dst, ss, rs):
        part = pl.ds(0, wall_count - 1)
        return pltpu.make_async_remote_copy(
            src_ref=src.at[part], dst_ref=dst.at[part], send_sem=ss,
            recv_sem=rs.at[0] if rs.shape else rs, device_id=dev(away(1)), device_id_type=MESH,
        )

    def send_turns(msg, lo, hi):
        @pl.loop(lo, hi)
        def _(j):
            to_owner(msg, turn(j))

    msg_a = (send_a, recv_a, a_ss, a_rs)
    msg_va = (vec_a, got_vec_a, va_ss, va_rs)
    msg_b = (send_b, recv_b, b_ss, b_rs)
    msg_vb = (vec_b, got_vec_b, vb_ss, vb_rs)
    msg_c = (c_out, c_in, c_ss, c_rs)
    msg_e = (e_out, e_in, e_ss, e_rs)
    msg_x = (x_out, x_in, x_ss, x_rs)

    small = [
        pltpu.make_async_copy(src, dst, small_sem.at[n])
        for n, (src, dst) in enumerate((
            (state_hbm, ext.at[1]), (source_hbm, source_ref), (coef_hbm, coef_ref),
            (nbr_hbm, nbr_ref), (lift_hbm, lift_ref), (slot_hbm, slot_ref),
        ))
    ]
    for copy in small:
        copy.start()
    for ks, first in (((0, 1), 1), ((2,), 0)):
        for n in range(first, 4):
            for k in ks:
                for e in range(2):
                    load(k, e, block(n)).start()

    tail_s[...] = jnp.zeros_like(tail_s)
    row = lax.broadcasted_iota(jnp.int32, (128, 128), 0)
    col = lax.broadcasted_iota(jnp.int32, (128, 128), 1)
    perm[...] = (col == 8 * lax.rem(row, 16) + row // 16).astype(F32).astype(BF)
    row = lax.broadcasted_iota(jnp.int32, (64, 16), 0)
    col = lax.broadcasted_iota(jnp.int32, (64, 16), 1)
    last[...] = (col == 8 * lax.rem(row, 8) + row // 8).astype(F32).astype(BF)

    def stored_product(t, a, b):
        return dot(t_hi[t, a], t_hi[t, b]) + (dot(t_hi[t, a], t_lo[t, b]) + dot(t_lo[t, a], t_hi[t, b]))

    def gather_lines(sources, b):
        for k, store in sources:
            for e in range(2):
                load(k, e, b).wait()

        @pl.loop(0, 2)
        def _(c):
            for t in range(5):
                first = pl.multiple_of(80 * c + 16 * t, 16)
                for k, store in sources:
                    for e in range(2):
                        x = raw[k, e, b, pl.ds(first, 16)].reshape(128, B)
                        y = dot(perm[...], x).astype(BF)
                        for u in range(8):
                            store[e, 8 * b + u, pl.ds(first, 16), :] = y[16 * u : 16 * u + 16]

        for k, store in sources:
            for e in range(2):
                x = raw[k, e, b, pl.ds(160, 2)].reshape(16, B)
                y = dot(last[...], x).astype(BF)
                for u in range(8):
                    store[e, 8 * b + u, pl.ds(160, 2), :] = y[8 * u : 8 * u + 2]

    def steps(b, right):
        for u in range(8):
            for e in range(2):
                t_hi[u, e], t_lo[u, e] = halves(dot(d_mat[e, 8 * b + u], right[e, 8 * b + u]))

    def fwd_maps(i, send):
        b = block(i)
        gather_lines(((0, d_mat), (1, l_mat)), b)
        steps(b, l_mat)

        for t in range(8):
            prod[t] = stored_product(t, 1, 0)
        for t in range(8):
            encode(prod[t], active(1, 8 * b + t), send_a, vec_a, 8 * b + t, t % 4)

        if send:
            @pl.loop(0, 8)
            def _(u):
                to_owner(msg_a, line(b, u))

    def back_maps(i):
        b = block(i)
        gather_lines(((2, u_mat),), b)
        steps(b, u_mat)

        for t in range(8):
            prod[t] = stored_product(t, 0, 1)
        for t in range(8):
            l = 8 * b + t
            v_mat[l] = t_hi[t, 1]
            b_mat[l] = prod[t].astype(BF)
            encode(prod[t], active(1, l), send_b, vec_b, l, t % 4)
            vec_b[l, pl.ds(0, 1), :] = jnp.zeros((1, B), F32)

    fwd_maps(0, False)

    for copy in small:
        copy.wait()
    pl.semaphore_wait(barrier, wall_count - 1 + 2)
    halo = []
    for k, (s, place) in enumerate(((after, 0), (before, 2))):
        copy = pltpu.make_async_remote_copy(
            src_ref=ext.at[1], dst_ref=ext.at[place], send_sem=ext_ss.at[k], recv_sem=ext_rs.at[k],
            device_id=(me, s), device_id_type=MESH,
        )
        copy.start()
        halo.append(copy)

    @pl.loop(1, 8)
    def _(u):
        to_owner(msg_a, line(block(0), u))

    recv_a[me] = send_a[mine]

    @pl.loop(1, 4)
    def _(i):
        fwd_maps(i, True)

    kpos = lax.broadcasted_iota(jnp.int32, (192, 64), 0)
    own = kpos == 64 + lax.broadcasted_iota(jnp.int32, (192, 64), 1)
    weight = jnp.zeros((192, 64), F32)
    for f in range(4):
        hit = kpos == nbr_ref[pl.ds(f, 1), :]
        weight = weight + coef_ref[pl.ds(f, 1), :] * (own.astype(F32) - hit.astype(F32))
    for copy in halo:
        copy.wait()
    w1 = weight.astype(BF)
    rest = weight - w1.astype(F32)
    w2 = rest.astype(BF)
    w3 = (rest - w2.astype(F32)).astype(BF)
    cells = ext[...].reshape(192, B)
    face_sum = sum(
        lax.dot_general(w, cells, TN, preferred_element_type=F32) for w in (w3, w2, w1)
    ).astype(BF)
    spos = lax.broadcasted_iota(jnp.int32, (64, 32), 0)
    for e in range(2):
        pick = (spos == slot_ref[pl.ds(e, 1), :]).astype(F32).astype(BF)
        faces = lax.dot_general(pick, face_sum, TN, preferred_element_type=F32).astype(BF)
        own_rows = lax.dot_general(pick, source_ref[...], TN, preferred_element_type=F32)
        rhs[e] = own_rows - dot(faces, lift_ref[...])

    @pl.loop(0, lines // 8)
    def _(i):
        ls = [turn(8 * i + t) for t in range(8)]
        y = [active(0, l) * apply_map(d_mat[0, l], wide(rhs[0, pl.ds(l, 1), :])) for l in ls]
        y = [wide(rhs[1, pl.ds(l, 1), :]) - apply_map(l_mat[1, l], v) for l, v in zip(ls, y)]
        y = [active(1, l) * apply_map(d_mat[1, l], v) for l, v in zip(ls, y)]
        for l, v in zip(ls, y):
            vec_a[l, pl.ds(0, 1), :] = v[:1]
        send_turns(msg_va, jnp.maximum(8 * i, 1), 8 * i + 8)

    got_vec_a[me] = vec_a[mine]

    def sender(j):
        return owner(8 * lax.rem(my_b - j // 8 + 4, 4) + lax.rem(my_u - j + 32, 8))

    def take(msg, i):
        @pl.loop(0, 4)
        def _(q):
            js = [8 * i + 2 * q + t for t in range(2)]
            for j in js:
                @pl.when(j > 0)
                def _():
                    arrive(msg, sender(j))
            for t, j in enumerate(js):
                decode(msg[1], sender(j), t)

    def send_back(lo, hi):
        @pl.loop(lo, hi)
        def _(j):
            to_owner(msg_b, turn(j))
            to_owner(msg_vb, turn(j))

    @pl.loop(0, 4)
    def _(i):
        back_maps(i)
        send_back(jnp.maximum(8 * i, 1), jnp.minimum(8 * i + 8, FIRST))
        take(msg_a, i)

    everyone(*msg_va).wait_recv()

    def send_group(msg, i):
        for t in range(8):
            @pl.when(8 * i + t != me)
            def _():
                to_device(msg, 8 * i + t)

    def fwd(i, v):
        for t in range(8):
            d = 8 * i + t
            c_out[d] = v[:1]
            got = got_vec_a[d]
            v = apply_coded(d, wide(got[1:2]), v) + wide(got[0:1])
        send_group(msg_c, i)
        return v

    lax.fori_loop(0, wall_count // 8, fwd, jnp.zeros((8, B), F32))
    c_in[mine] = c_out[me]

    send_back(FIRST, wall_count)

    everyone(*msg_c).wait_recv()

    @pl.loop(0, lines // 8)
    def _(i):
        ls = [turn(8 * i + t) for t in range(8)]
        v = [wide(rhs[0, pl.ds(l, 1), :]) - apply_map(l_mat[0, l], wide(c_in[l])) for l in ls]
        first = [active(0, l) * apply_map(d_mat[0, l], v) for l, v in zip(ls, v)]
        v = [wide(rhs[1, pl.ds(l, 1), :]) - apply_map(l_mat[1, l], y) for l, y in zip(ls, first)]
        second = [active(1, l) * apply_map(d_mat[1, l], v) for l, v in zip(ls, v)]
        for l, y in zip(ls, second):
            y_s[1, l] = y
        v = [apply_map(u_mat[0, l], y) for l, y in zip(ls, second)]
        v = [active(0, l) * apply_map(d_mat[0, l], v) for l, v in zip(ls, v)]
        for l, y, e in zip(ls, first, v):
            e_out[l] = y[:1] - e[:1]
        send_turns(msg_e, jnp.maximum(8 * i, 1), 8 * i + 8)

    e_in[me] = e_out[mine]

    recv_b[me] = send_b[mine]
    got_vec_b[me] = vec_b[mine]

    @pl.loop(0, 4)
    def _(i):
        take(msg_b, i)

    everyone(*msg_vb).wait_recv()
    everyone(*msg_e).wait_recv()

    def bwd(k, v):
        i = wall_count // 8 - 1 - k
        for t in reversed(range(8)):
            d = 8 * i + t
            x_out[d] = v[:1]
            got = got_vec_b[d]
            v = apply_coded(d, wide(got[1:2]), v) + wide(e_in[d])
        send_group(msg_x, i)
        return v

    lax.fori_loop(0, wall_count // 8, bwd, jnp.zeros((8, B), F32))
    x_in[mine] = x_out[me]

    everyone(*msg_x).wait_recv()

    @pl.loop(0, lines // 8)
    def _(i):
        ls = [turn(8 * i + t) for t in range(8)]
        v = [apply_map(v_mat[l], wide(x_in[l])) for l in ls]
        w = [apply_map(b_mat[l], wide(x_in[l])) for l in ls]
        for l, v, w in zip(ls, v, w):
            out_ref[1, pl.ds(l, 1), :] = y_s[1, l][:1] - active(1, l) * v[:1]
            out_ref[0, pl.ds(l, 1), :] = e_out[l] + active(1, l) * w[:1]

    for msg in (msg_a, msg_va, msg_b, msg_vb, msg_c, msg_e, msg_x):
        everyone(*msg).wait_send()


def per_device(state, source, face_coef, neighbour, lift, elem_slot, line_len, dinv, lower, upper):
    wall = lax.axis_size("wall")
    lines = dinv.shape[1]
    vmem = pl.BlockSpec(memory_space=pltpu.VMEM)
    hbm = pl.BlockSpec(memory_space=pl.ANY)
    raw = pltpu.VMEM((3, 2, 4, B, 8, B), BF)
    mat = pltpu.VMEM((2, lines, B, B), BF)
    coded = pltpu.VMEM((wall, CODED, 128), jnp.int16)
    vec = pltpu.VMEM((wall, 2, B), F32)
    row = pltpu.VMEM((wall, 1, B), F32)
    sems = pltpu.SemaphoreType.DMA((wall,))
    one = pltpu.SemaphoreType.DMA
    turned = [jnp.transpose(m, (0, 2, 1, 3)) for m in (dinv, lower, upper)]
    return pl.pallas_call(
        kernel,
        out_shape=jax.ShapeDtypeStruct((2, lines, B), F32),
        in_specs=[hbm] * 6 + [pl.BlockSpec(memory_space=pltpu.SMEM)] + [hbm] * 3,
        out_specs=vmem,
        scratch_shapes=[
            pltpu.VMEM((64, B), BF), pltpu.VMEM((4, 64), F32), pltpu.VMEM((4, 64), jnp.int32),
            pltpu.VMEM((B, B), BF), pltpu.VMEM((2, lines), jnp.int32),
            pltpu.VMEM((lines, B, B), BF), pltpu.VMEM((lines, B, B), BF),
            raw,
            pltpu.VMEM((128, 128), BF), pltpu.VMEM((64, 16), BF),
            pltpu.VMEM((8, B, B), F32),
            pltpu.VMEM((8, 2, B, B), BF), pltpu.VMEM((8, 2, B, B), BF),
            mat, mat, mat,
            pltpu.VMEM((3, 64, B), BF),
            pltpu.VMEM((2, 32, B), F32),
            pltpu.VMEM((4, 168, 128), F32),
            coded, coded, vec, vec, coded, coded, vec, vec,
            pltpu.VMEM((wall, B, B), BF), pltpu.VMEM((wall, B, B), BF),
            pltpu.VMEM((2, lines, 8, B), F32),
            row, row, row, row, row, row,
            pltpu.SemaphoreType.DMA((6,)),
            pltpu.SemaphoreType.DMA((3, 2, 4)),
            pltpu.SemaphoreType.DMA((2,)), pltpu.SemaphoreType.DMA((2,)),
        ] + [one, sems, one, one, one, sems] + [one] * 8,
        compiler_params=pltpu.CompilerParams(
            collective_id=0, has_side_effects=True, vmem_limit_bytes=67043328
        ),
        name="lines",
    )(state, source, face_coef.T, neighbour.T, lift, elem_slot, line_len, *turned)


def solution(mesh):
    in_specs = (
        P(("wall", "surf"), None),
        P(("wall", "surf"), None),
        P(("wall", "surf"), None),
        P(("wall", "surf"), None),
        P(),
        P("wall", "surf"),
        P("surf"),
        P("wall", "surf", None, None),
        P("wall", "surf", None, None),
        P("wall", "surf", None, None),
    )
    return jax.shard_map(
        per_device, mesh=mesh, in_specs=in_specs, out_specs=P("wall", "surf", None), check_vma=False
    )
```
